256 devices in a mesh: lon: 32 (over y, x, core), lat: 4 (over z_hi), comp: 2 (over z_lo).
Axes of the slice: x: 4, y: 4, z: 8 (z_hi: 4, z_lo: 2; z = z_hi * 2 + z_lo), core: 2. Of those that a mesh axis runs over, the one named last changes fastest.
Arguments:
- ocean_state: float32 [4, 80, 256, 1024], P(None, None, 'lon', ('lat', 'comp')), may hold values from -6 to 6
- level_count: int32 [256, 1024], P('lon', ('lat', 'comp')), may hold values from 0 to 80, as said below
- mix_rate: float32 [80, 256, 1024], P(None, 'lon', ('lat', 'comp')), may hold values from 0.05 to 5
- atmos_flux: bfloat16 [8, 1024, 4, 256], P(('lat', 'comp'), 'lon'), may hold values from -6 to 6
- remap_weight: bfloat16 [8, 1024, 256, 128], P(('lat', 'comp'), 'lon'), may hold values from -0.375 to 0.375
- remap_target: int32 [8, 1024], P(('lat', 'comp'), 'lon'), may hold values from 0 to 31, as said below
- remap_slot: int32 [8, 1024], P(('lat', 'comp'), 'lon'), may hold values from 0 to 7
Outputs:
- ocean_next: float32 [4, 80, 256, 1024], P(None, None, 'lon', ('lat', 'comp'))
The draws below stay inside these ranges and needn't reach their ends.
Inputs may be any that keep to these rules, and one draw needn't show every extreme that they name: `level_count`: 0 marks a land column. `remap_target`: among the blocks of one device each longitude tile index appears exactly 1 times.
All inputs are finite; a program needn't handle non-finite values.
Results may differ from the reference program's by a relative error of at most 0.0003.
Values sent between devices are 32-bit elements; how exact they have to be, the bound alone decides.
A program may use at most 128 MiB of HBM per device.

```python
import math
import jax
import jax.numpy as jnp
from jax import lax

LON_DEV = 8
LAT_DEV = 128
LEVELS = 80
FLUXES = 4
BLOCK_CELLS = 256
SEND_BLOCKS = 1
SUBSTEPS = 2
BLOCKS_DEV = 32
LAT_TILES = 8
LON_CELLS = 256
LAT_CELLS = 1024
N_LON = 32


def draw_level_count(key, part):
    raw_levels = jax.random.randint(key, (LON_CELLS, LAT_CELLS), -(LEVELS // 3), LEVELS + 1)
    return jnp.maximum(raw_levels, 0).astype(jnp.int32)


def shuffled_blocks(device_key):
    return jax.random.permutation(device_key, BLOCKS_DEV)


def draw_remap_target(key, part):
    device_keys = jax.random.split(key, LAT_TILES * N_LON)
    orders = jax.vmap(shuffled_blocks)(device_keys)
    return (orders // SEND_BLOCKS).reshape(LAT_TILES, N_LON * BLOCKS_DEV).astype(jnp.int32)


def with_ends(values, key, smallest, high):
    shape = values.shape
    place = [jax.random.randint(jax.random.fold_in(key, axis), (), 0, shape[axis]) for axis in range(len(shape))]
    values = values.at[tuple(place)].set(smallest)
    longest = shape.index(max(shape))
    place[longest] = (place[longest] + 1) % shape[longest]
    return values.at[tuple(place)].set(high)


def shard_levels(key, shape, cuts, least, largest):
    def one(axis_at, blocks):
        steps = jax.random.uniform(jax.random.fold_in(jax.random.fold_in(key, 6), axis_at), (blocks,), jnp.float32, least / len(cuts), largest / len(cuts))
        return jnp.repeat(jnp.exp(steps), shape[axis_at] // blocks).reshape((-1,) + (1,) * (len(shape) - axis_at - 1))

    level = one(*cuts[0])
    for cut in cuts[1:]:
        level = level * one(*cut)
    return level


def centred(key, extent, scale, most, cuts=(), held_as=jnp.bfloat16):
    gain = shard_levels(key, extent, cuts, -0.22, 0.18) if cuts else 1.0
    values = jax.random.normal(key, extent, jnp.float32) * scale * gain
    return jnp.minimum(jnp.maximum(values, -most), most).astype(held_as)


def setup_inputs(seed: int = 0) -> dict:
    keys = jax.random.split(jax.random.key(seed), 8)
    ocean_state = centred(keys[0], (4, LEVELS, LON_CELLS, LAT_CELLS), 1.0, 6.0, ((2, 32), (3, 8)), jnp.float32)
    level_count = draw_level_count(jax.random.fold_in(keys[7], 71), 0)
    mix_rate = jnp.clip(jnp.exp(math.log(5.0) - 4.6051702 * jax.random.uniform(keys[2], (LEVELS, LON_CELLS, LAT_CELLS), jnp.float32) ** shard_levels(keys[2], (LEVELS, LON_CELLS, LAT_CELLS), ((1, 32), (2, 8)), -0.2, 0.2)), 0.05, 5.0)
    atmos_flux = centred(keys[3], (LAT_TILES, N_LON * BLOCKS_DEV, FLUXES, BLOCK_CELLS), 1.0, 6.0, ((0, 8), (1, 32)))
    remap_weight = centred(keys[4], (LAT_TILES, N_LON * BLOCKS_DEV, BLOCK_CELLS, LAT_DEV), BLOCK_CELLS ** -0.5, 0.375, ((0, 8), (1, 32)))
    remap_target = draw_remap_target(jax.random.fold_in(keys[7], 71), 0)
    remap_slot = with_ends(jax.random.randint(keys[6], (LAT_TILES, N_LON * BLOCKS_DEV), 0, LON_DEV), jax.random.fold_in(keys[6], 1), 0, LON_DEV - 1).astype(jnp.int32)
    return dict(ocean_state=ocean_state, level_count=level_count, mix_rate=mix_rate, atmos_flux=atmos_flux, remap_weight=remap_weight, remap_target=remap_target, remap_slot=remap_slot)


DIFFUSE = 0.2
VISCOUS = 0.2
ADVECTION = 0.5
THERMAL = 0.2
HALINE = 0.15
GRAVITY = 0.05
CORIOLIS = 0.3
SURFACE_GAIN = (0.5, 0.4, 0.6, 0.6)


def centre_of(values):
    return values[..., 1:-1, 1:-1]


def east_of(values):
    return values[..., 2:, 1:-1]


def west_of(values):
    return values[..., :-2, 1:-1]


def north_of(values):
    return values[..., 1:-1, 2:]


def south_of(values):
    return values[..., 1:-1, :-2]


def laplace(values, wet_padded):
    middle = centre_of(values)
    total = east_of(wet_padded) * (east_of(values) - middle)
    total = total + west_of(wet_padded) * (west_of(values) - middle)
    total = total + north_of(wet_padded) * (north_of(values) - middle)
    total = total + south_of(wet_padded) * (south_of(values) - middle)
    return total


def vertical_mix(tendency, rate, wet_mask):
    level_total = tendency.shape[1]
    coupling = rate[:-1] * wet_mask[:-1] * wet_mask[1:]
    zero_level = jnp.zeros_like(rate[:1])
    upper = jnp.concatenate([coupling, zero_level], axis=0)
    lower = jnp.concatenate([zero_level, coupling], axis=0)
    diagonal = 1.0 + upper + lower
    ratio_list = []
    value_list = []
    prev_ratio = jnp.zeros_like(rate[0])
    prev_value = jnp.zeros_like(tendency[:, 0])
    for level_at in range(level_total):
        pivot = diagonal[level_at] + lower[level_at] * prev_ratio
        prev_ratio = -upper[level_at] / pivot
        prev_value = (tendency[:, level_at] + lower[level_at] * prev_value) / pivot
        ratio_list.append(prev_ratio)
        value_list.append(prev_value)
    following = prev_value
    solved = [following]
    for level_at in range(level_total - 2, -1, -1):
        following = value_list[level_at] - ratio_list[level_at] * following
        solved.append(following)
    return jnp.stack(solved[::-1], axis=1)


def baroclinic(state_padded, rate_padded, count_padded, forcing, first_row, lat_total):
    level_total = state_padded.shape[1]
    level_ids = jnp.arange(level_total, dtype=jnp.int32).astype(jnp.float32)[:, None, None]
    wet_padded = (level_ids < count_padded[None]).astype(jnp.float32)
    masked = state_padded * wet_padded[None]
    wet_mask = centre_of(wet_padded)
    tracers = masked[:2]
    u_padded = masked[2]
    v_padded = masked[3]
    u_middle = centre_of(u_padded)
    v_middle = centre_of(v_padded)
    carried = u_middle * (east_of(tracers) - west_of(tracers)) + v_middle * (north_of(tracers) - south_of(tracers))
    tracer_next = centre_of(tracers) + DIFFUSE * laplace(tracers, wet_padded) - 0.5 * ADVECTION * carried
    density = HALINE * masked[1] - THERMAL * masked[0]
    pressure = GRAVITY * jnp.cumsum(density, axis=0) * wet_padded
    force_x = 0.5 * (east_of(pressure) - west_of(pressure))
    force_y = 0.5 * (north_of(pressure) - south_of(pressure))
    row_count = wet_mask.shape[-1]
    row_ids = (first_row + jnp.arange(row_count, dtype=jnp.int32)).astype(jnp.float32)
    rotation = CORIOLIS * (2.0 * (row_ids + 0.5) / lat_total - 1.0)
    u_next = u_middle + VISCOUS * laplace(u_padded, wet_padded) + rotation * v_middle - force_x
    v_next = v_middle + VISCOUS * laplace(v_padded, wet_padded) - rotation * u_middle - force_y
    updated = jnp.stack([tracer_next[0], tracer_next[1], u_next, v_next])
    gains = jnp.array(SURFACE_GAIN, dtype=jnp.float32)[:, None, None]
    surface = updated[:, 0] + gains * forcing
    updated = jnp.concatenate([surface[:, None], updated[:, 1:]], axis=1) * wet_mask[None]
    return vertical_mix(updated, centre_of(rate_padded), wet_mask) * wet_mask[None]


def pad_grid(values):
    wrapped = jnp.concatenate([values[..., -1:, :], values, values[..., :1, :]], axis=-2)
    widths = [(0, 0)] * (values.ndim - 1) + [(1, 1)]
    return jnp.pad(wrapped, widths)


def remap_tile(pieces):
    flux_block, weight_block, target_tile, slot_index = pieces
    partial_value = jnp.einsum('bfc,bco->bfo', flux_block.astype(jnp.float32), weight_block.astype(jnp.float32), precision=lax.Precision.HIGHEST)
    column = target_tile * LON_DEV + slot_index
    return jax.ops.segment_sum(partial_value, column, num_segments=LON_CELLS)


def reference(ocean_state, level_count, mix_rate, atmos_flux, remap_weight, remap_target, remap_slot):
    tiles = lax.map(remap_tile, (atmos_flux, remap_weight, remap_target, remap_slot))
    forcing = jnp.transpose(tiles, (2, 1, 0, 3)).reshape(FLUXES, LON_CELLS, LAT_CELLS)
    rate_padded = pad_grid(mix_rate)
    count_padded = pad_grid(level_count.astype(jnp.float32))
    state = ocean_state
    for step_index in range(SUBSTEPS):
        state = baroclinic(pad_grid(state), rate_padded, count_padded, forcing, 0, LAT_CELLS)
    return state
```

```python
import functools

import jax
import jax.numpy as jnp
from jax import lax
from jax.experimental import pallas as pl
from jax.experimental.pallas import tpu as pltpu
from jax.sharding import PartitionSpec as P

DIFFUSE = 0.2
ADVECTION = 0.5
THERMAL = 0.2
HALINE = 0.15
GRAVITY = 0.05
CORIOLIS = 0.3
SURFACE_GAIN = (0.5, 0.4, 0.6, 0.6)

FIELDS = 4
ROWS = 8
LANES = 128
CHUNKS = 4
UNROLL = 4
MSG = FIELDS + 1
MESH = pl.DeviceIdType.MESH


def window(
    n_lon, n_lat, n_comp, levels,
    state, count, rate, flux, weight, target, slot, out,
    raw, cnt, rt, fx, wt, tg, sl,
    grid_q, north_send, row_e, row_w, halo_e, halo_w, halo_n, halo_s, merged,
    part, outbox, inbox, force,
    c0_ref, ib_ref, ab_ref, bb_ref, it_ref, at_ref, bt_ref,
    val, res,
    in_sem, out_sem, halo_send_sem, halo_recv_sem, msg_sem,
):
    per = levels // CHUNKS
    me = lax.axis_index("lon")
    depth = lax.axis_index("lat") * n_comp + lax.axis_index("comp")
    total = n_lat * n_comp
    east = lax.rem(me + 1, n_lon)
    west = lax.rem(me + n_lon - 1, n_lon)
    north = lax.rem(depth + 1, total)
    south = lax.rem(depth + total - 1, total)

    def lon_id(where):
        return {"lon": where}

    def lat_id(where):
        return {"lat": where // n_comp, "comp": lax.rem(where, n_comp)}

    cnt_in = pltpu.make_async_copy(count, cnt, in_sem.at[0])
    cnt_in.start()
    raw_in = []
    for c in range(CHUNKS):
        copy = pltpu.make_async_copy(
            state.at[:, pl.ds(c * per, per)], raw.at[:, pl.ds(c * per, per)], in_sem.at[1 + c]
        )
        copy.start()
        raw_in.append(copy)
    rest_in = []
    for i, (a, b) in enumerate(((target, tg), (slot, sl), (flux, fx), (weight, wt), (rate, rt))):
        copy = pltpu.make_async_copy(a, b, in_sem.at[1 + CHUNKS + i])
        copy.start()
        rest_in.append(copy)

    barrier = pltpu.get_barrier_semaphore()
    pl.semaphore_signal(barrier, inc=1, device_id=lat_id(north), device_id_type=MESH)
    pl.semaphore_signal(barrier, inc=1, device_id=lat_id(south), device_id_type=MESH)

    def greet(d, carry):
        pl.semaphore_signal(
            barrier, inc=1, device_id=lon_id(lax.rem(me + d, n_lon)), device_id_type=MESH
        )
        return carry

    lax.fori_loop(1, n_lon, greet, 0)

    lane = lax.broadcasted_iota(jnp.int32, (ROWS, LANES), 1)
    row = lax.broadcasted_iota(jnp.int32, (ROWS, LANES), 0)
    first_lane, last_lane = lane == 0, lane == LANES - 1
    first_row, last_row = row == 0, row == ROWS - 1
    lane_half = lane // 2
    zero = jnp.zeros((ROWS, LANES), jnp.float32)

    def halo_copies(step, c):
        lo = ROWS + c * FIELDS * per
        size = FIELDS * per
        if step == 0 and c == 0:
            lo, size = 0, size + ROWS
        rows = pl.ds(lo, size)
        made = []
        for i, (src, dst, where) in enumerate((
            (row_e.at[step, rows], halo_w.at[step, rows], lon_id(east)),
            (row_w.at[step, rows], halo_e.at[step, rows], lon_id(west)),
            (north_send.at[step, c], halo_s.at[step, c], lat_id(north)),
            (north_send.at[step, c], halo_n.at[step, c], lat_id(south)),
        )):
            made.append(pltpu.make_async_remote_copy(
                src_ref=src,
                dst_ref=dst,
                send_sem=halo_send_sem.at[step, c, i],
                recv_sem=halo_recv_sem.at[step, c, i],
                device_id=where,
                device_id_type=MESH,
            ))
        return made

    def pack(step, c, kk, fields, packed):
        at = ROWS + (c * per + kk) * FIELDS
        made = []
        for f in range(FIELDS):
            q = fields[f]
            base = ROWS + ((c * per + kk) * FIELDS + f) * ROWS
            grid_q[step, pl.ds(pl.multiple_of(base, ROWS), ROWS), :] = q
            row_w[step, pl.ds(at + f, 1), :] = q[0:1, :]
            row_e[step, pl.ds(at + f, 1), :] = q[ROWS - 1:ROWS, :]
            turned = pltpu.roll(q, 2 * kk + 1, 1)
            made.append(jnp.where(lane_half == kk, turned, packed[f]))
        return tuple(made)

    cnt_in.wait()
    wet_count = cnt[...]
    wet_count_f = wet_count.astype(jnp.float32)
    for step in range(2):
        grid_q[step, pl.ds(0, ROWS), :] = zero
        grid_q[step, pl.ds(ROWS + levels * FIELDS * ROWS, ROWS), :] = zero
    row_w[0, pl.ds(0, ROWS), :] = jnp.broadcast_to(wet_count_f[0:1, :], (ROWS, LANES))
    row_e[0, pl.ds(0, ROWS), :] = jnp.broadcast_to(wet_count_f[ROWS - 1:, :], (ROWS, LANES))
    sends = []
    for c in range(CHUNKS):
        raw_in[c].wait()

        def pack_raw(kk, packed):
            k = c * per + kk
            wet = k < wet_count
            fields = [jnp.where(wet, raw[f, k], zero) for f in range(FIELDS)]
            return pack(0, c, kk, fields, packed)

        packed = lax.fori_loop(0, per, pack_raw, (zero,) * FIELDS, unroll=UNROLL)
        for f in range(FIELDS):
            tile = packed[f]
            if c == 0 and f == 0:
                turned = pltpu.roll(wet_count_f, 2 * per + 1, 1)
                tile = jnp.where(lane_half == per, turned, tile)
            north_send[0, c, f] = tile
        if c == 0:
            pl.semaphore_wait(barrier, n_lon + 1)
        for copy in halo_copies(0, c):
            copy.start()
            sends.append(copy)

    rest_in[0].wait()
    rest_in[1].wait()
    rest_in[2].wait()
    rest_in[3].wait()

    def one_block(b, carry):
        part[b] = jnp.dot(fx[b], wt[b], preferred_element_type=jnp.float32)
        return carry

    lax.fori_loop(0, n_lon, one_block, 0, unroll=UNROLL)
    chosen = (
        lax.broadcasted_iota(jnp.int32, (n_lon, n_lon), 0)
        == jnp.broadcast_to(tg[...], (n_lon, n_lon))
    )
    pick = jnp.where(chosen, 1.0, 0.0).astype(jnp.float32)
    slot_f = jnp.broadcast_to(sl[...].astype(jnp.float32), (n_lon, n_lon))
    for f in range(FIELDS):
        outbox[:, f, :] = jnp.dot(
            pick, part[:, f, :], precision=lax.Precision.HIGHEST,
            preferred_element_type=jnp.float32,
        )
    outbox[:, FIELDS, :] = jnp.dot(
        jnp.where(chosen, slot_f, 0.0), jnp.ones((n_lon, LANES), jnp.float32),
        precision=lax.Precision.HIGHEST, preferred_element_type=jnp.float32,
    )

    def post(d, carry):
        owner = lax.rem(me + d, n_lon)
        pltpu.make_async_remote_copy(
            src_ref=outbox.at[owner],
            dst_ref=inbox.at[me],
            send_sem=msg_sem.at[0],
            recv_sem=msg_sem.at[1],
            device_id=lon_id(owner),
            device_id_type=MESH,
        ).start()
        return carry

    lax.fori_loop(1, n_lon, post, 0)

    rest_in[4].wait()

    def across(k):
        return jnp.where(k + 1 < wet_count, rt[k], zero)

    def factor(i, carry):
        below, inv_b, above, inv_t = carry
        k = levels - 1 - i
        upper = across(jnp.maximum(k - 1, 0))
        upper = jnp.where(k > 0, upper, 0.0)
        inv_b = 1.0 / (1.0 + upper + below - below * below * inv_b)
        masked = jnp.where(k < wet_count, inv_b, 0.0)
        ib_ref[k] = masked
        ab_ref[k] = below * masked
        bb_ref[k] = jnp.where(k > 0, upper, 1.0) * masked
        lower = jnp.where(i < levels - 1, across(i), 0.0)
        inv_t = 1.0 / (1.0 + above + lower - above * above * inv_t)
        masked = jnp.where(i < wet_count, inv_t, 0.0)
        it_ref[i] = masked
        at_ref[i] = jnp.where(i > 0, above, 1.0) * masked
        bt_ref[i] = lower * masked
        return upper, inv_b, lower, inv_t

    lax.fori_loop(0, levels, factor, (zero,) * 4, unroll=UNROLL)

    odd = lax.rem(lane, 2) == 1
    no_north, no_south = depth == total - 1, depth == 0

    def arrive(step, c):
        for copy in halo_copies(step, c):
            copy.wait_recv()
        for f in range(FIELDS):
            from_north = jnp.where(no_north, 0.0, halo_n[step, c, f])
            from_south = jnp.where(no_south, 0.0, halo_s[step, c, f])
            merged[f] = jnp.where(odd, from_north, from_south)

    def lat_pair(q, tile, kk):
        edge = pltpu.roll(tile, LANES - 1 - 2 * kk, 1)
        n = pltpu.roll(jnp.where(first_lane, edge, q), LANES - 1, 1)
        s = pltpu.roll(jnp.where(last_lane, edge, q), 1, 1)
        return n, s

    def row_of(ref, step, at):
        return jnp.broadcast_to(ref[step, pl.ds(at, 1), :], (ROWS, LANES))

    y = (depth * LANES + lane).astype(jnp.float32)
    turning = CORIOLIS * (2.0 * (y + 0.5) / (total * LANES) - 1.0)

    def tendency(step, c, kk, sums, counts):
        k = c * per + kk
        at = ROWS + k * FIELDS
        mid, e, w, n, s = [], [], [], [], []
        for f in range(FIELDS):
            base = ROWS + (k * FIELDS + f) * ROWS
            q = grid_q[step, pl.ds(pl.multiple_of(base, ROWS), ROWS), :]
            e.append(jnp.where(last_row, row_of(halo_e, step, at + f), pltpu.roll(q, ROWS - 1, 0)))
            w.append(jnp.where(first_row, row_of(halo_w, step, at + f), pltpu.roll(q, 1, 0)))
            up, down = lat_pair(q, merged[f], kk)
            n.append(up)
            s.append(down)
            mid.append(q)
        wets = [k < a for a in counts]
        if step == 0:
            shares = [jnp.where(m, DIFFUSE, 0.0) for m in wets]
            c0 = (1.0 - (shares[0] + shares[1])) - (shares[2] + shares[3])
            c0_ref[k] = c0
        else:
            c0 = c0_ref[k]
        half = 0.5 * ADVECTION
        a, b = half * mid[2], half * mid[3]
        to_e, to_w, to_n, to_s = DIFFUSE - a, DIFFUSE + a, DIFFUSE - b, DIFFUSE + b
        new = []
        for f in range(2):
            new.append(
                c0 * mid[f]
                + ((to_e * e[f] + to_w * w[f]) + (to_n * n[f] + to_s * s[f]))
            )
        scale = 0.5 * GRAVITY
        made, pressures = [], []
        for side, m, total_d in zip((e, w, n, s), wets, sums):
            total_d = total_d + (scale * HALINE * side[1] - scale * THERMAL * side[0])
            made.append(total_d)
            pressures.append(jnp.where(m, total_d, 0.0))
        for f, sign, lo, hi in ((2, 1, 1, 0), (3, -1, 3, 2)):
            spread = DIFFUSE * ((e[f] + w[f]) + (n[f] + s[f]))
            twist = turning * mid[5 - f]
            base = c0 * mid[f] + spread
            base = base + twist if sign > 0 else base - twist
            new.append(base - (pressures[hi] - pressures[lo]))
        return new, tuple(made)

    arrive(0, 0)
    count_e = jnp.where(last_row, halo_e[0, pl.ds(0, ROWS), :], pltpu.roll(wet_count_f, ROWS - 1, 0))
    count_w = jnp.where(first_row, halo_w[0, pl.ds(0, ROWS), :], pltpu.roll(wet_count_f, 1, 0))
    count_n, count_s = lat_pair(wet_count_f, merged[0], per)
    counts = [a.astype(jnp.int32) for a in (count_e, count_w, count_n, count_s)]
    sums = (zero,) * 4
    for c in range(CHUNKS):
        if c > 0:
            arrive(0, c)

        def first(kk, sums):
            new, sums = tendency(0, c, kk, sums, counts)
            k = c * per + kk
            ib = ib_ref[k]
            for f in range(FIELDS):
                val[k, f] = ib * new[f]
            return sums

        sums = lax.fori_loop(0, per, first, sums, unroll=UNROLL)

    def upward(i, carry):
        k = levels - 1 - i
        ab = ab_ref[k]
        made = tuple(val[k, f] + ab * carry[f] for f in range(FIELDS))
        for f in range(FIELDS):
            val[k, f] = made[f]
        return made

    lax.fori_loop(0, levels, upward, (zero,) * FIELDS, unroll=UNROLL)

    inbox[me] = outbox[me]
    pltpu.make_async_copy(
        inbox.at[pl.ds(0, n_lon - 1)], inbox.at[pl.ds(0, n_lon - 1)], msg_sem.at[1]
    ).wait()
    row_f = row.astype(jnp.float32)

    def receive(s, carry):
        hit = row_f == jnp.broadcast_to(inbox[s, pl.ds(FIELDS, 1), :], (ROWS, LANES))
        return tuple(
            carry[f]
            + jnp.where(hit, jnp.broadcast_to(inbox[s, pl.ds(f, 1), :], (ROWS, LANES)), 0.0)
            for f in range(FIELDS)
        )

    forced = lax.fori_loop(0, n_lon, receive, (zero,) * FIELDS, unroll=UNROLL)
    for f in range(FIELDS):
        force[f] = SURFACE_GAIN[f] * forced[f]

    carry = tuple(force[f] for f in range(FIELDS))
    for c in range(CHUNKS):

        def downward(kk, carry):
            before, packed = carry
            k = c * per + kk
            bb = bb_ref[k]
            made = tuple(val[k, f] + bb * before[f] for f in range(FIELDS))
            return made, pack(1, c, kk, made, packed)

        carry, packed = lax.fori_loop(0, per, downward, (carry, (zero,) * FIELDS), unroll=UNROLL)
        for f in range(FIELDS):
            north_send[1, c, f] = packed[f]
        for copy in halo_copies(1, c):
            copy.start()
            sends.append(copy)

    sums = (zero,) * 4
    carry = tuple(force[f] for f in range(FIELDS))
    for c in range(CHUNKS):
        arrive(1, c)

        def second(kk, state_in):
            sums, before = state_in
            new, sums = tendency(1, c, kk, sums, counts)
            k = c * per + kk
            it, at = it_ref[k], at_ref[k]
            made = tuple(it * new[f] + at * before[f] for f in range(FIELDS))
            for f in range(FIELDS):
                val[k, f] = made[f]
            return sums, made

        sums, carry = lax.fori_loop(0, per, second, (sums, carry), unroll=UNROLL)

    carry = (zero,) * FIELDS
    outs = []
    for c in reversed(range(CHUNKS)):

        def settle(i, carry):
            k = c * per + per - 1 - i
            bt = bt_ref[k]
            made = tuple(val[k, f] + bt * carry[f] for f in range(FIELDS))
            for f in range(FIELDS):
                res[f, k] = made[f]
            return made

        carry = lax.fori_loop(0, per, settle, carry, unroll=UNROLL)
        copy = pltpu.make_async_copy(
            res.at[:, pl.ds(c * per, per)], out.at[:, pl.ds(c * per, per)], out_sem.at[c]
        )
        copy.start()
        outs.append(copy)
    for copy in outs:
        copy.wait()
    for copy in sends:
        copy.wait_send()
    pltpu.make_async_copy(
        outbox.at[pl.ds(0, n_lon - 1)], outbox.at[pl.ds(0, n_lon - 1)], msg_sem.at[0]
    ).wait()


def local(ocean_state, level_count, mix_rate, atmos_flux, remap_weight, remap_target, remap_slot):
    fields, levels, rows, lanes = ocean_state.shape
    n_lon, n_lat, n_comp = (lax.axis_size(a) for a in ("lon", "lat", "comp"))
    blocks, cells = atmos_flux.shape[1], atmos_flux.shape[3]
    per = levels // CHUNKS
    tile = (levels, rows, lanes)
    f32 = jnp.float32
    row_shape = (2, ROWS + levels * fields, lanes)
    lat_shape = (2, CHUNKS, fields, rows, lanes)
    anywhere = pl.BlockSpec(memory_space=pl.ANY)
    return pl.pallas_call(
        functools.partial(window, n_lon, n_lat, n_comp, levels),
        out_shape=jax.ShapeDtypeStruct(ocean_state.shape, f32),
        in_specs=[anywhere] * 7,
        out_specs=anywhere,
        scratch_shapes=[
            pltpu.VMEM(ocean_state.shape, f32),
            pltpu.VMEM((rows, lanes), jnp.int32),
            pltpu.VMEM(tile, f32),
            pltpu.VMEM((blocks, fields, cells), jnp.bfloat16),
            pltpu.VMEM((blocks, cells, lanes), jnp.bfloat16),
            pltpu.VMEM((1, blocks), jnp.int32),
            pltpu.VMEM((1, blocks), jnp.int32),
            pltpu.VMEM((2, levels * fields * rows + 2 * rows, lanes), f32),
            pltpu.VMEM(lat_shape, f32),
            pltpu.VMEM(row_shape, f32),
            pltpu.VMEM(row_shape, f32),
            pltpu.VMEM(row_shape, f32),
            pltpu.VMEM(row_shape, f32),
            pltpu.VMEM(lat_shape, f32),
            pltpu.VMEM(lat_shape, f32),
            pltpu.VMEM((fields, rows, lanes), f32),
            pltpu.VMEM((blocks, fields, lanes), f32),
            pltpu.VMEM((n_lon, MSG, lanes), f32),
            pltpu.VMEM((n_lon, MSG, lanes), f32),
            pltpu.VMEM((fields, rows, lanes), f32),
        ]
        + [pltpu.VMEM(tile, f32)] * 7
        + [
            pltpu.VMEM((levels, fields, rows, lanes), f32),
            pltpu.VMEM(ocean_state.shape, f32),
            pltpu.SemaphoreType.DMA((1 + CHUNKS + 5,)),
            pltpu.SemaphoreType.DMA((CHUNKS,)),
            pltpu.SemaphoreType.DMA((2, CHUNKS, 4)),
            pltpu.SemaphoreType.DMA((2, CHUNKS, 4)),
            pltpu.SemaphoreType.DMA((2,)),
        ],
        compiler_params=pltpu.CompilerParams(
            collective_id=0, has_side_effects=True, vmem_limit_bytes=48 << 20
        ),
        cost_estimate=pl.CostEstimate(flops=20_000_000, bytes_accessed=5_200_000, transcendentals=0),
    )(
        ocean_state, level_count, mix_rate, atmos_flux[0], remap_weight[0], remap_target, remap_slot
    )


def solution(mesh):
    placed = (
        P(None, None, "lon", ("lat", "comp")),
        P("lon", ("lat", "comp")),
        P(None, "lon", ("lat", "comp")),
        P(("lat", "comp"), "lon", None, None),
        P(("lat", "comp"), "lon", None, None),
        P(("lat", "comp"), "lon"),
        P(("lat", "comp"), "lon"),
    )
    return jax.shard_map(
        local,
        mesh=mesh,
        in_specs=placed,
        out_specs=P(None, None, "lon", ("lat", "comp")),
        check_vma=False,
    )
```

```python
import functools

import jax
import jax.numpy as jnp
from jax import lax
from jax.experimental import pallas as pl
from jax.experimental.pallas import tpu as pltpu
from jax.sharding import PartitionSpec as P

DIFFUSE = 0.2
ADVECTION = 0.5
THERMAL = 0.2
HALINE = 0.15
GRAVITY = 0.05
CORIOLIS = 0.3
SURFACE_GAIN = (0.5, 0.4, 0.6, 0.6)

FIELDS = 4
ROWS = 8
LANES = 128
CHUNKS = 4
UNROLL = 10
MSG = FIELDS + 1
MESH = pl.DeviceIdType.MESH


def window(
    n_lon, n_lat, n_comp, levels,
    state, count, rate, flux, weight, target, slot, out,
    raw, cnt, rt, fx, wt, tg, sl,
    grid_q, north_send, row_e, row_w, halo_e, halo_w, halo_n, halo_s, merged,
    part, outbox, inbox, force,
    c0_ref, ib_ref, ab_ref, bb_ref, it_ref, at_ref, bt_ref,
    val,
    in_sem, halo_send_sem, halo_recv_sem, msg_sem,
):
    per = levels // CHUNKS
    me = lax.axis_index("lon")
    depth = lax.axis_index("lat") * n_comp + lax.axis_index("comp")
    total = n_lat * n_comp
    east = lax.rem(me + 1, n_lon)
    west = lax.rem(me + n_lon - 1, n_lon)
    north = jnp.minimum(depth + 1, total - 1)
    south = jnp.maximum(depth - 1, 0)

    def lon_id(where):
        return {"lon": where}

    def lat_id(where):
        return {"lat": where // n_comp, "comp": lax.rem(where, n_comp)}

    cnt_in = pltpu.make_async_copy(count, cnt, in_sem.at[0])
    cnt_in.start()
    raw_in = []
    for c in range(CHUNKS):
        copy = pltpu.make_async_copy(
            state.at[:, pl.ds(c * per, per)], raw.at[:, pl.ds(c * per, per)], in_sem.at[1 + c]
        )
        copy.start()
        raw_in.append(copy)
    rest_in = []
    for i, (a, b) in enumerate(((target, tg), (slot, sl), (flux, fx), (weight, wt), (rate, rt))):
        copy = pltpu.make_async_copy(a, b, in_sem.at[1 + CHUNKS + i])
        copy.start()
        rest_in.append(copy)

    barrier = pltpu.get_barrier_semaphore()
    has_north, has_south = depth < total - 1, depth > 0

    @pl.when(jnp.logical_not(has_north))
    def _():
        halo_n[...] = jnp.zeros_like(halo_n)

    @pl.when(jnp.logical_not(has_south))
    def _():
        halo_s[...] = jnp.zeros_like(halo_s)

    @pl.when(has_north)
    def _():
        pl.semaphore_signal(barrier, inc=1, device_id=lat_id(north), device_id_type=MESH)

    @pl.when(has_south)
    def _():
        pl.semaphore_signal(barrier, inc=1, device_id=lat_id(south), device_id_type=MESH)

    def greet(d, carry):
        pl.semaphore_signal(
            barrier, inc=1, device_id=lon_id(lax.rem(me + d, n_lon)), device_id_type=MESH
        )
        return carry

    lax.fori_loop(1, n_lon, greet, 0)

    lane = lax.broadcasted_iota(jnp.int32, (ROWS, LANES), 1)
    row = lax.broadcasted_iota(jnp.int32, (ROWS, LANES), 0)
    first_lane, last_lane = lane == 0, lane == LANES - 1
    first_row, last_row = row == 0, row == ROWS - 1
    lane_half = lane // 2
    zero = jnp.zeros((ROWS, LANES), jnp.float32)

    def halo_copies(step, c):
        lo = ROWS + c * FIELDS * per
        size = FIELDS * per
        if step == 0 and c == 0:
            lo, size = 0, size + ROWS
        rows = pl.ds(lo, size)
        made = []
        for i, (src, dst, where) in enumerate((
            (row_e.at[step, rows], halo_w.at[step, rows], lon_id(east)),
            (row_w.at[step, rows], halo_e.at[step, rows], lon_id(west)),
            (north_send.at[step, c], halo_s.at[step, c], lat_id(north)),
            (north_send.at[step, c], halo_n.at[step, c], lat_id(south)),
        )):
            made.append(pltpu.make_async_remote_copy(
                src_ref=src,
                dst_ref=dst,
                send_sem=halo_send_sem.at[step, c, i],
                recv_sem=halo_recv_sem.at[step, c, i],
                device_id=where,
                device_id_type=MESH,
            ))
        return made

    def on_sides(made, act):
        act(made[0])
        act(made[1])

        @pl.when(has_north)
        def _():
            act(made[2])

        @pl.when(has_south)
        def _():
            act(made[3])

    def send_halos(step, c):
        on_sides(halo_copies(step, c), lambda copy: copy.start())

    def pack(step, c, kk, fields, packed):
        at = ROWS + (c * per + kk) * FIELDS
        made = []
        for f in range(FIELDS):
            q = fields[f]
            base = ROWS + ((c * per + kk) * FIELDS + f) * ROWS
            grid_q[step, pl.ds(pl.multiple_of(base, ROWS), ROWS), :] = q
            row_w[step, pl.ds(at + f, 1), :] = q[0:1, :]
            row_e[step, pl.ds(at + f, 1), :] = q[ROWS - 1:ROWS, :]
            turned = pltpu.roll(q, 2 * kk + 1, 1)
            made.append(jnp.where(lane_half == kk, turned, packed[f]))
        return tuple(made)

    cnt_in.wait()
    wet_count = cnt[...]
    wet_count_f = wet_count.astype(jnp.float32)
    for step in range(2):
        grid_q[step, pl.ds(0, ROWS), :] = zero
        grid_q[step, pl.ds(ROWS + levels * FIELDS * ROWS, ROWS), :] = zero
    row_w[0, pl.ds(0, ROWS), :] = jnp.broadcast_to(wet_count_f[0:1, :], (ROWS, LANES))
    row_e[0, pl.ds(0, ROWS), :] = jnp.broadcast_to(wet_count_f[ROWS - 1:, :], (ROWS, LANES))
    for c in range(CHUNKS):
        raw_in[c].wait()

        def pack_raw(kk, packed):
            k = c * per + kk
            wet = k < wet_count
            fields = [jnp.where(wet, raw[f, k], zero) for f in range(FIELDS)]
            return pack(0, c, kk, fields, packed)

        packed = lax.fori_loop(0, per, pack_raw, (zero,) * FIELDS, unroll=UNROLL)
        for f in range(FIELDS):
            tile = packed[f]
            if c == 0 and f == 0:
                turned = pltpu.roll(wet_count_f, 2 * per + 1, 1)
                tile = jnp.where(lane_half == per, turned, tile)
            north_send[0, c, f] = tile
        if c == 0:
            met = n_lon - 1 + has_north.astype(jnp.int32) + has_south.astype(jnp.int32)
            pl.semaphore_wait(barrier, met)
        send_halos(0, c)

    rest_in[0].wait()
    rest_in[1].wait()
    rest_in[2].wait()
    rest_in[3].wait()

    def one_block(b, carry):
        part[b] = jnp.dot(fx[b], wt[b], preferred_element_type=jnp.float32)
        return carry

    lax.fori_loop(0, n_lon, one_block, 0, unroll=UNROLL)
    chosen = (
        lax.broadcasted_iota(jnp.int32, (n_lon, n_lon), 0)
        == jnp.broadcast_to(tg[...], (n_lon, n_lon))
    )
    pick = jnp.where(chosen, 1.0, 0.0).astype(jnp.float32)
    slot_f = jnp.broadcast_to(sl[...].astype(jnp.float32), (n_lon, n_lon))
    for f in range(FIELDS):
        outbox[:, f, :] = jnp.dot(
            pick, part[:, f, :], precision=lax.Precision.HIGHEST,
            preferred_element_type=jnp.float32,
        )
    outbox[:, FIELDS, :] = jnp.dot(
        jnp.where(chosen, slot_f, 0.0), jnp.ones((n_lon, LANES), jnp.float32),
        precision=lax.Precision.HIGHEST, preferred_element_type=jnp.float32,
    )

    def post(d, carry):
        owner = lax.rem(me + d, n_lon)
        pltpu.make_async_remote_copy(
            src_ref=outbox.at[owner],
            dst_ref=inbox.at[me],
            send_sem=msg_sem.at[0],
            recv_sem=msg_sem.at[1],
            device_id=lon_id(owner),
            device_id_type=MESH,
        ).start()
        return carry

    lax.fori_loop(1, n_lon, post, 0)

    rest_in[4].wait()

    def across(k):
        return jnp.where(k + 1 < wet_count, rt[k], zero)

    def factor(i, carry):
        below, inv_b, above, inv_t = carry
        k = levels - 1 - i
        upper = across(jnp.maximum(k - 1, 0))
        upper = jnp.where(k > 0, upper, 0.0)
        inv_b = 1.0 / (1.0 + upper + below - below * below * inv_b)
        masked = jnp.where(k < wet_count, inv_b, 0.0)
        ib_ref[k] = masked
        ab_ref[k] = below * masked
        bb_ref[k] = jnp.where(k > 0, upper, 1.0) * masked
        lower = jnp.where(i < levels - 1, across(i), 0.0)
        inv_t = 1.0 / (1.0 + above + lower - above * above * inv_t)
        masked = jnp.where(i < wet_count, inv_t, 0.0)
        it_ref[i] = masked
        at_ref[i] = jnp.where(i > 0, above, 1.0) * masked
        bt_ref[i] = lower * masked
        return upper, inv_b, lower, inv_t

    lax.fori_loop(0, levels, factor, (zero,) * 4, unroll=UNROLL)

    odd = lax.rem(lane, 2) == 1

    def arrive(step, c):
        made = halo_copies(step, c)
        made[0].wait_recv()
        made[1].wait_recv()

        @pl.when(has_south)
        def _():
            made[2].wait_recv()

        @pl.when(has_north)
        def _():
            made[3].wait_recv()

        for f in range(FIELDS):
            merged[f] = jnp.where(odd, halo_n[step, c, f], halo_s[step, c, f])

    def lat_pair(q, tile, kk):
        edge = pltpu.roll(tile, LANES - 1 - 2 * kk, 1)
        n = pltpu.roll(jnp.where(first_lane, edge, q), LANES - 1, 1)
        s = pltpu.roll(jnp.where(last_lane, edge, q), 1, 1)
        return n, s

    def row_of(ref, step, at):
        return jnp.broadcast_to(ref[step, pl.ds(at, 1), :], (ROWS, LANES))

    y = (depth * LANES + lane).astype(jnp.float32)
    turning = CORIOLIS * (2.0 * (y + 0.5) / (total * LANES) - 1.0)

    def tendency(step, c, kk, sums, counts):
        k = c * per + kk
        at = ROWS + k * FIELDS
        mid, e, w, n, s = [], [], [], [], []
        for f in range(FIELDS):
            base = ROWS + (k * FIELDS + f) * ROWS
            q = grid_q[step, pl.ds(pl.multiple_of(base, ROWS), ROWS), :]
            e.append(jnp.where(last_row, row_of(halo_e, step, at + f), pltpu.roll(q, ROWS - 1, 0)))
            w.append(jnp.where(first_row, row_of(halo_w, step, at + f), pltpu.roll(q, 1, 0)))
            up, down = lat_pair(q, merged[f], kk)
            n.append(up)
            s.append(down)
            mid.append(q)
        wets = [k < a for a in counts]
        if step == 0:
            shares = [jnp.where(m, DIFFUSE, 0.0) for m in wets]
            c0 = (1.0 - (shares[0] + shares[1])) - (shares[2] + shares[3])
            c0_ref[k] = c0
        else:
            c0 = c0_ref[k]
        half = 0.5 * ADVECTION
        a, b = half * mid[2], half * mid[3]
        to_e, to_w, to_n, to_s = DIFFUSE - a, DIFFUSE + a, DIFFUSE - b, DIFFUSE + b
        new = []
        for f in range(2):
            new.append(
                c0 * mid[f]
                + ((to_e * e[f] + to_w * w[f]) + (to_n * n[f] + to_s * s[f]))
            )
        scale = 0.5 * GRAVITY
        made, pressures = [], []
        for side, m, total_d in zip((e, w, n, s), wets, sums):
            total_d = total_d + (scale * HALINE * side[1] - scale * THERMAL * side[0])
            made.append(total_d)
            pressures.append(jnp.where(m, total_d, 0.0))
        for f, sign, lo, hi in ((2, 1, 1, 0), (3, -1, 3, 2)):
            spread = DIFFUSE * ((e[f] + w[f]) + (n[f] + s[f]))
            twist = turning * mid[5 - f]
            base = c0 * mid[f] + spread
            base = base + twist if sign > 0 else base - twist
            new.append(base - (pressures[hi] - pressures[lo]))
        return new, tuple(made)

    arrive(0, 0)
    count_e = jnp.where(last_row, halo_e[0, pl.ds(0, ROWS), :], pltpu.roll(wet_count_f, ROWS - 1, 0))
    count_w = jnp.where(first_row, halo_w[0, pl.ds(0, ROWS), :], pltpu.roll(wet_count_f, 1, 0))
    count_n, count_s = lat_pair(wet_count_f, merged[0], per)
    counts = [a.astype(jnp.int32) for a in (count_e, count_w, count_n, count_s)]
    sums = (zero,) * 4
    for c in range(CHUNKS):
        if c > 0:
            arrive(0, c)

        def first(kk, sums):
            new, sums = tendency(0, c, kk, sums, counts)
            k = c * per + kk
            ib = ib_ref[k]
            for f in range(FIELDS):
                val[k, f] = ib * new[f]
            return sums

        sums = lax.fori_loop(0, per, first, sums, unroll=UNROLL)

    def upward(i, carry):
        k = levels - 1 - i
        ab = ab_ref[k]
        made = tuple(val[k, f] + ab * carry[f] for f in range(FIELDS))
        for f in range(FIELDS):
            val[k, f] = made[f]
        return made

    lax.fori_loop(0, levels, upward, (zero,) * FIELDS, unroll=UNROLL)

    inbox[me] = outbox[me]
    pltpu.make_async_copy(
        inbox.at[pl.ds(0, n_lon - 1)], inbox.at[pl.ds(0, n_lon - 1)], msg_sem.at[1]
    ).wait()
    row_f = row.astype(jnp.float32)

    def receive(s, carry):
        hit = row_f == jnp.broadcast_to(inbox[s, pl.ds(FIELDS, 1), :], (ROWS, LANES))
        return tuple(
            carry[f]
            + jnp.where(hit, jnp.broadcast_to(inbox[s, pl.ds(f, 1), :], (ROWS, LANES)), 0.0)
            for f in range(FIELDS)
        )

    forced = lax.fori_loop(0, n_lon, receive, (zero,) * FIELDS, unroll=UNROLL)
    for f in range(FIELDS):
        force[f] = SURFACE_GAIN[f] * forced[f]

    carry = tuple(force[f] for f in range(FIELDS))
    for c in range(CHUNKS):

        def downward(kk, carry):
            before, packed = carry
            k = c * per + kk
            bb = bb_ref[k]
            made = tuple(val[k, f] + bb * before[f] for f in range(FIELDS))
            return made, pack(1, c, kk, made, packed)

        carry, packed = lax.fori_loop(0, per, downward, (carry, (zero,) * FIELDS), unroll=UNROLL)
        for f in range(FIELDS):
            north_send[1, c, f] = packed[f]
        send_halos(1, c)

    sums = (zero,) * 4
    carry = tuple(force[f] for f in range(FIELDS))
    for c in range(CHUNKS):
        arrive(1, c)

        def second(kk, state_in):
            sums, before = state_in
            new, sums = tendency(1, c, kk, sums, counts)
            k = c * per + kk
            it, at = it_ref[k], at_ref[k]
            made = tuple(it * new[f] + at * before[f] for f in range(FIELDS))
            for f in range(FIELDS):
                val[k, f] = made[f]
            return sums, made

        sums, carry = lax.fori_loop(0, per, second, (sums, carry), unroll=UNROLL)

    carry = (zero,) * FIELDS
    for c in reversed(range(CHUNKS)):

        def settle(i, carry):
            k = c * per + per - 1 - i
            bt = bt_ref[k]
            made = tuple(val[k, f] + bt * carry[f] for f in range(FIELDS))
            for f in range(FIELDS):
                out[f, k] = made[f]
            return made

        carry = lax.fori_loop(0, per, settle, carry, unroll=UNROLL)
    for step in range(2):
        for c in range(CHUNKS):
            on_sides(halo_copies(step, c), lambda copy: copy.wait_send())
    pltpu.make_async_copy(
        outbox.at[pl.ds(0, n_lon - 1)], outbox.at[pl.ds(0, n_lon - 1)], msg_sem.at[0]
    ).wait()


def local(ocean_state, level_count, mix_rate, atmos_flux, remap_weight, remap_target, remap_slot):
    fields, levels, rows, lanes = ocean_state.shape
    n_lon, n_lat, n_comp = (lax.axis_size(a) for a in ("lon", "lat", "comp"))
    blocks, cells = atmos_flux.shape[1], atmos_flux.shape[3]
    per = levels // CHUNKS
    tile = (levels, rows, lanes)
    f32 = jnp.float32
    row_shape = (2, ROWS + levels * fields, lanes)
    lat_shape = (2, CHUNKS, fields, rows, lanes)
    anywhere = pl.BlockSpec(memory_space=pltpu.HBM)
    return pl.pallas_call(
        functools.partial(window, n_lon, n_lat, n_comp, levels),
        out_shape=jax.ShapeDtypeStruct(ocean_state.shape, f32),
        in_specs=[anywhere] * 7,
        out_specs=pl.BlockSpec(memory_space=pltpu.VMEM),
        scratch_shapes=[
            pltpu.VMEM(ocean_state.shape, f32),
            pltpu.VMEM((rows, lanes), jnp.int32),
            pltpu.VMEM(tile, f32),
            pltpu.VMEM((blocks, fields, cells), jnp.bfloat16),
            pltpu.VMEM((blocks, cells, lanes), jnp.bfloat16),
            pltpu.VMEM((1, blocks), jnp.int32),
            pltpu.VMEM((1, blocks), jnp.int32),
            pltpu.VMEM((2, levels * fields * rows + 2 * rows, lanes), f32),
            pltpu.VMEM(lat_shape, f32),
            pltpu.VMEM(row_shape, f32),
            pltpu.VMEM(row_shape, f32),
            pltpu.VMEM(row_shape, f32),
            pltpu.VMEM(row_shape, f32),
            pltpu.VMEM(lat_shape, f32),
            pltpu.VMEM(lat_shape, f32),
            pltpu.VMEM((fields, rows, lanes), f32),
            pltpu.VMEM((blocks, fields, lanes), f32),
            pltpu.VMEM((n_lon, MSG, lanes), f32),
            pltpu.VMEM((n_lon, MSG, lanes), f32),
            pltpu.VMEM((fields, rows, lanes), f32),
        ]
        + [pltpu.VMEM(tile, f32)] * 7
        + [
            pltpu.VMEM((levels, fields, rows, lanes), f32),
            pltpu.SemaphoreType.DMA((1 + CHUNKS + 5,)),
            pltpu.SemaphoreType.DMA((2, CHUNKS, 4)),
            pltpu.SemaphoreType.DMA((2, CHUNKS, 4)),
            pltpu.SemaphoreType.DMA((2,)),
        ],
        compiler_params=pltpu.CompilerParams(
            collective_id=0, has_side_effects=True, vmem_limit_bytes=60 << 20
        ),
        cost_estimate=pl.CostEstimate(flops=20_000_000, bytes_accessed=5_200_000, transcendentals=0),
    )(
        ocean_state, level_count, mix_rate, atmos_flux[0], remap_weight[0], remap_target, remap_slot
    )


def solution(mesh):
    placed = (
        P(None, None, "lon", ("lat", "comp")),
        P("lon", ("lat", "comp")),
        P(None, "lon", ("lat", "comp")),
        P(("lat", "comp"), "lon", None, None),
        P(("lat", "comp"), "lon", None, None),
        P(("lat", "comp"), "lon"),
        P(("lat", "comp"), "lon"),
    )
    return jax.shard_map(
        local,
        mesh=mesh,
        in_specs=placed,
        out_specs=P(None, None, "lon", ("lat", "comp")),
        check_vma=False,
    )
```

```python
import functools

import jax
import jax.numpy as jnp
from jax import lax
from jax.experimental import pallas as pl
from jax.experimental.pallas import tpu as pltpu
from jax.sharding import PartitionSpec as P

DIFFUSE = 0.2
ADVECTION = 0.5
THERMAL = 0.2
HALINE = 0.15
GRAVITY = 0.05
CORIOLIS = 0.3
SURFACE_GAIN = (0.5, 0.4, 0.6, 0.6)

FIELDS = 4
ROWS = 8
LANES = 128
CHUNKS = 4
UNROLL = 10
MSG = FIELDS + 1
MESH = pl.DeviceIdType.MESH


def window(
    n_lon, n_lat, n_comp, levels,
    state, count, rate, flux, weight, target, slot, out,
    raw, cnt, rt, fx, wt, tg, sl,
    grid_q, north_send, row_e, row_w, halo_e, halo_w, halo_n, halo_s, merged,
    part, outbox, inbox, force,
    c0_ref, ib_ref, ab_ref, bb_ref, it_ref, at_ref, bt_ref,
    val,
    in_sem, halo_send_sem, halo_recv_sem, msg_sem,
):
    per = levels // CHUNKS
    me = lax.axis_index("lon")
    depth = lax.axis_index("lat") * n_comp + lax.axis_index("comp")
    total = n_lat * n_comp
    east = lax.rem(me + 1, n_lon)
    west = lax.rem(me + n_lon - 1, n_lon)
    north = jnp.minimum(depth + 1, total - 1)
    south = jnp.maximum(depth - 1, 0)

    def lon_id(where):
        return {"lon": where}

    def lat_id(where):
        return {"lat": where // n_comp, "comp": lax.rem(where, n_comp)}

    cnt_in = pltpu.make_async_copy(count, cnt, in_sem.at[0])
    cnt_in.start()
    raw_in = []
    for c in range(CHUNKS):
        copy = pltpu.make_async_copy(
            state.at[:, pl.ds(c * per, per)], raw.at[:, pl.ds(c * per, per)], in_sem.at[1 + c]
        )
        copy.start()
        raw_in.append(copy)
    barrier = pltpu.get_barrier_semaphore()
    has_north, has_south = depth < total - 1, depth > 0

    @pl.when(jnp.logical_not(has_north))
    def _():
        halo_n[...] = jnp.zeros_like(halo_n)

    @pl.when(jnp.logical_not(has_south))
    def _():
        halo_s[...] = jnp.zeros_like(halo_s)

    @pl.when(has_north)
    def _():
        pl.semaphore_signal(barrier, inc=1, device_id=lat_id(north), device_id_type=MESH)

    @pl.when(has_south)
    def _():
        pl.semaphore_signal(barrier, inc=1, device_id=lat_id(south), device_id_type=MESH)

    def greet(d, carry):
        pl.semaphore_signal(
            barrier, inc=1, device_id=lon_id(lax.rem(me + d, n_lon)), device_id_type=MESH
        )
        return carry

    lax.fori_loop(1, n_lon, greet, 0)

    lane = lax.broadcasted_iota(jnp.int32, (ROWS, LANES), 1)
    row = lax.broadcasted_iota(jnp.int32, (ROWS, LANES), 0)
    first_lane, last_lane = lane == 0, lane == LANES - 1
    first_row, last_row = row == 0, row == ROWS - 1
    lane_half = lane // 2
    zero = jnp.zeros((ROWS, LANES), jnp.float32)

    def halo_copies(step, c):
        lo = ROWS + c * FIELDS * per
        size = FIELDS * per
        if step == 0 and c == 0:
            lo, size = 0, size + ROWS
        rows = pl.ds(lo, size)
        made = []
        for i, (src, dst, where) in enumerate((
            (row_e.at[step, rows], halo_w.at[step, rows], lon_id(east)),
            (row_w.at[step, rows], halo_e.at[step, rows], lon_id(west)),
            (north_send.at[step, c], halo_s.at[step, c], lat_id(north)),
            (north_send.at[step, c], halo_n.at[step, c], lat_id(south)),
        )):
            made.append(pltpu.make_async_remote_copy(
                src_ref=src,
                dst_ref=dst,
                send_sem=halo_send_sem.at[step, c, i],
                recv_sem=halo_recv_sem.at[step, c, i],
                device_id=where,
                device_id_type=MESH,
            ))
        return made

    def on_sides(made, act):
        act(made[0])
        act(made[1])

        @pl.when(has_north)
        def _():
            act(made[2])

        @pl.when(has_south)
        def _():
            act(made[3])

    def send_halos(step, c):
        on_sides(halo_copies(step, c), lambda copy: copy.start())

    def pack(step, c, kk, fields, packed):
        at = ROWS + (c * per + kk) * FIELDS
        made = []
        for f in range(FIELDS):
            q = fields[f]
            base = ROWS + ((c * per + kk) * FIELDS + f) * ROWS
            grid_q[step, pl.ds(pl.multiple_of(base, ROWS), ROWS), :] = q
            row_w[step, pl.ds(at + f, 1), :] = q[0:1, :]
            row_e[step, pl.ds(at + f, 1), :] = q[ROWS - 1:ROWS, :]
            turned = pltpu.roll(q, 2 * kk + 1, 1)
            made.append(jnp.where(lane_half == kk, turned, packed[f]))
        return tuple(made)

    cnt_in.wait()
    wet_count = cnt[...]
    wet_count_f = wet_count.astype(jnp.float32)
    for step in range(2):
        grid_q[step, pl.ds(0, ROWS), :] = zero
        grid_q[step, pl.ds(ROWS + levels * FIELDS * ROWS, ROWS), :] = zero
    row_w[0, pl.ds(0, ROWS), :] = jnp.broadcast_to(wet_count_f[0:1, :], (ROWS, LANES))
    row_e[0, pl.ds(0, ROWS), :] = jnp.broadcast_to(wet_count_f[ROWS - 1:, :], (ROWS, LANES))
    for c in range(CHUNKS):
        raw_in[c].wait()
        if c == 0:
            rest_in = []
            for i, (a, b) in enumerate(((target, tg), (slot, sl), (flux, fx), (weight, wt), (rate, rt))):
                copy = pltpu.make_async_copy(a, b, in_sem.at[1 + CHUNKS + i])
                copy.start()
                rest_in.append(copy)


        def pack_raw(kk, packed):
            k = c * per + kk
            wet = k < wet_count
            fields = [jnp.where(wet, raw[f, k], zero) for f in range(FIELDS)]
            return pack(0, c, kk, fields, packed)

        packed = lax.fori_loop(0, per, pack_raw, (zero,) * FIELDS, unroll=UNROLL)
        for f in range(FIELDS):
            tile = packed[f]
            if c == 0 and f == 0:
                turned = pltpu.roll(wet_count_f, 2 * per + 1, 1)
                tile = jnp.where(lane_half == per, turned, tile)
            north_send[0, c, f] = tile
        if c == 0:
            met = n_lon - 1 + has_north.astype(jnp.int32) + has_south.astype(jnp.int32)
            pl.semaphore_wait(barrier, met)
        send_halos(0, c)

    rest_in[0].wait()
    rest_in[1].wait()
    rest_in[2].wait()
    rest_in[3].wait()

    def one_block(b, carry):
        part[b] = jnp.dot(fx[b], wt[b], preferred_element_type=jnp.float32)
        return carry

    lax.fori_loop(0, n_lon, one_block, 0, unroll=UNROLL)
    chosen = (
        lax.broadcasted_iota(jnp.int32, (n_lon, n_lon), 0)
        == jnp.broadcast_to(tg[...], (n_lon, n_lon))
    )
    pick = jnp.where(chosen, 1.0, 0.0).astype(jnp.float32)
    slot_f = jnp.broadcast_to(sl[...].astype(jnp.float32), (n_lon, n_lon))
    for f in range(FIELDS):
        outbox[:, f, :] = jnp.dot(
            pick, part[:, f, :], precision=lax.Precision.HIGHEST,
            preferred_element_type=jnp.float32,
        )
    outbox[:, FIELDS, :] = jnp.dot(
        jnp.where(chosen, slot_f, 0.0), jnp.ones((n_lon, LANES), jnp.float32),
        precision=lax.Precision.HIGHEST, preferred_element_type=jnp.float32,
    )

    def post(d, carry):
        owner = lax.rem(me + d, n_lon)
        pltpu.make_async_remote_copy(
            src_ref=outbox.at[owner],
            dst_ref=inbox.at[me],
            send_sem=msg_sem.at[0],
            recv_sem=msg_sem.at[1],
            device_id=lon_id(owner),
            device_id_type=MESH,
        ).start()
        return carry

    lax.fori_loop(1, n_lon, post, 0)

    rest_in[4].wait()

    def across(k):
        return jnp.where(k + 1 < wet_count, rt[k], zero)

    def factor(i, carry):
        below, inv_b, above, inv_t = carry
        k = levels - 1 - i
        upper = across(jnp.maximum(k - 1, 0))
        upper = jnp.where(k > 0, upper, 0.0)
        inv_b = 1.0 / (1.0 + upper + below - below * below * inv_b)
        masked = jnp.where(k < wet_count, inv_b, 0.0)
        ib_ref[k] = masked
        ab_ref[k] = below * masked
        bb_ref[k] = jnp.where(k > 0, upper, 1.0) * masked
        lower = jnp.where(i < levels - 1, across(i), 0.0)
        inv_t = 1.0 / (1.0 + above + lower - above * above * inv_t)
        masked = jnp.where(i < wet_count, inv_t, 0.0)
        it_ref[i] = masked
        at_ref[i] = jnp.where(i > 0, above, 1.0) * masked
        bt_ref[i] = lower * masked
        return upper, inv_b, lower, inv_t

    lax.fori_loop(0, levels, factor, (zero,) * 4, unroll=UNROLL)

    odd = lax.rem(lane, 2) == 1

    def arrive(step, c):
        made = halo_copies(step, c)
        made[0].wait_recv()
        made[1].wait_recv()

        @pl.when(has_south)
        def _():
            made[2].wait_recv()

        @pl.when(has_north)
        def _():
            made[3].wait_recv()

        for f in range(FIELDS):
            merged[f] = jnp.where(odd, halo_n[step, c, f], halo_s[step, c, f])

    def lat_pair(q, tile, kk):
        edge = pltpu.roll(tile, LANES - 1 - 2 * kk, 1)
        n = pltpu.roll(jnp.where(first_lane, edge, q), LANES - 1, 1)
        s = pltpu.roll(jnp.where(last_lane, edge, q), 1, 1)
        return n, s

    def row_of(ref, step, at):
        return jnp.broadcast_to(ref[step, pl.ds(at, 1), :], (ROWS, LANES))

    y = (depth * LANES + lane).astype(jnp.float32)
    turning = CORIOLIS * (2.0 * (y + 0.5) / (total * LANES) - 1.0)

    def tendency(step, c, kk, sums, counts):
        k = c * per + kk
        at = ROWS + k * FIELDS
        mid, e, w, n, s = [], [], [], [], []
        for f in range(FIELDS):
            base = ROWS + (k * FIELDS + f) * ROWS
            q = grid_q[step, pl.ds(pl.multiple_of(base, ROWS), ROWS), :]
            e.append(jnp.where(last_row, row_of(halo_e, step, at + f), pltpu.roll(q, ROWS - 1, 0)))
            w.append(jnp.where(first_row, row_of(halo_w, step, at + f), pltpu.roll(q, 1, 0)))
            up, down = lat_pair(q, merged[f], kk)
            n.append(up)
            s.append(down)
            mid.append(q)
        wets = [k < a for a in counts]
        if step == 0:
            shares = [jnp.where(m, DIFFUSE, 0.0) for m in wets]
            c0 = (1.0 - (shares[0] + shares[1])) - (shares[2] + shares[3])
            c0_ref[k] = c0
        else:
            c0 = c0_ref[k]
        half = 0.5 * ADVECTION
        a, b = half * mid[2], half * mid[3]
        to_e, to_w, to_n, to_s = DIFFUSE - a, DIFFUSE + a, DIFFUSE - b, DIFFUSE + b
        new = []
        for f in range(2):
            new.append(
                c0 * mid[f]
                + ((to_e * e[f] + to_w * w[f]) + (to_n * n[f] + to_s * s[f]))
            )
        scale = 0.5 * GRAVITY
        made, pressures = [], []
        for side, m, total_d in zip((e, w, n, s), wets, sums):
            total_d = total_d + (scale * HALINE * side[1] - scale * THERMAL * side[0])
            made.append(total_d)
            pressures.append(jnp.where(m, total_d, 0.0))
        for f, sign, lo, hi in ((2, 1, 1, 0), (3, -1, 3, 2)):
            spread = DIFFUSE * ((e[f] + w[f]) + (n[f] + s[f]))
            twist = turning * mid[5 - f]
            base = c0 * mid[f] + spread
            base = base + twist if sign > 0 else base - twist
            new.append(base - (pressures[hi] - pressures[lo]))
        return new, tuple(made)

    arrive(0, 0)
    count_e = jnp.where(last_row, halo_e[0, pl.ds(0, ROWS), :], pltpu.roll(wet_count_f, ROWS - 1, 0))
    count_w = jnp.where(first_row, halo_w[0, pl.ds(0, ROWS), :], pltpu.roll(wet_count_f, 1, 0))
    count_n, count_s = lat_pair(wet_count_f, merged[0], per)
    counts = [a.astype(jnp.int32) for a in (count_e, count_w, count_n, count_s)]
    sums = (zero,) * 4
    for c in range(CHUNKS):
        if c > 0:
            arrive(0, c)

        def first(kk, sums):
            new, sums = tendency(0, c, kk, sums, counts)
            k = c * per + kk
            ib = ib_ref[k]
            for f in range(FIELDS):
                val[k, f] = ib * new[f]
            return sums

        sums = lax.fori_loop(0, per, first, sums, unroll=UNROLL)

    def upward(i, carry):
        k = levels - 1 - i
        ab = ab_ref[k]
        made = tuple(val[k, f] + ab * carry[f] for f in range(FIELDS))
        for f in range(FIELDS):
            val[k, f] = made[f]
        return made

    lax.fori_loop(0, levels, upward, (zero,) * FIELDS, unroll=UNROLL)

    inbox[me] = outbox[me]
    pltpu.make_async_copy(
        inbox.at[pl.ds(0, n_lon - 1)], inbox.at[pl.ds(0, n_lon - 1)], msg_sem.at[1]
    ).wait()
    row_f = row.astype(jnp.float32)

    def receive(s, carry):
        hit = row_f == jnp.broadcast_to(inbox[s, pl.ds(FIELDS, 1), :], (ROWS, LANES))
        return tuple(
            carry[f]
            + jnp.where(hit, jnp.broadcast_to(inbox[s, pl.ds(f, 1), :], (ROWS, LANES)), 0.0)
            for f in range(FIELDS)
        )

    forced = lax.fori_loop(0, n_lon, receive, (zero,) * FIELDS, unroll=UNROLL)
    for f in range(FIELDS):
        force[f] = SURFACE_GAIN[f] * forced[f]

    carry = tuple(force[f] for f in range(FIELDS))
    for c in range(CHUNKS):

        def downward(kk, carry):
            before, packed = carry
            k = c * per + kk
            bb = bb_ref[k]
            made = tuple(val[k, f] + bb * before[f] for f in range(FIELDS))
            return made, pack(1, c, kk, made, packed)

        carry, packed = lax.fori_loop(0, per, downward, (carry, (zero,) * FIELDS), unroll=UNROLL)
        for f in range(FIELDS):
            north_send[1, c, f] = packed[f]
        send_halos(1, c)

    sums = (zero,) * 4
    carry = tuple(force[f] for f in range(FIELDS))
    for c in range(CHUNKS):
        arrive(1, c)

        def second(kk, state_in):
            sums, before = state_in
            new, sums = tendency(1, c, kk, sums, counts)
            k = c * per + kk
            it, at = it_ref[k], at_ref[k]
            made = tuple(it * new[f] + at * before[f] for f in range(FIELDS))
            for f in range(FIELDS):
                val[k, f] = made[f]
            return sums, made

        sums, carry = lax.fori_loop(0, per, second, (sums, carry), unroll=UNROLL)

    carry = (zero,) * FIELDS
    for c in reversed(range(CHUNKS)):

        def settle(i, carry):
            k = c * per + per - 1 - i
            bt = bt_ref[k]
            made = tuple(val[k, f] + bt * carry[f] for f in range(FIELDS))
            for f in range(FIELDS):
                out[f, k] = made[f]
            return made

        carry = lax.fori_loop(0, per, settle, carry, unroll=UNROLL)
    for step in range(2):
        for c in range(CHUNKS):
            on_sides(halo_copies(step, c), lambda copy: copy.wait_send())
    pltpu.make_async_copy(
        outbox.at[pl.ds(0, n_lon - 1)], outbox.at[pl.ds(0, n_lon - 1)], msg_sem.at[0]
    ).wait()


def local(ocean_state, level_count, mix_rate, atmos_flux, remap_weight, remap_target, remap_slot):
    fields, levels, rows, lanes = ocean_state.shape
    n_lon, n_lat, n_comp = (lax.axis_size(a) for a in ("lon", "lat", "comp"))
    blocks, cells = atmos_flux.shape[1], atmos_flux.shape[3]
    per = levels // CHUNKS
    tile = (levels, rows, lanes)
    f32 = jnp.float32
    row_shape = (2, ROWS + levels * fields, lanes)
    lat_shape = (2, CHUNKS, fields, rows, lanes)
    anywhere = pl.BlockSpec(memory_space=pltpu.HBM)
    return pl.pallas_call(
        functools.partial(window, n_lon, n_lat, n_comp, levels),
        out_shape=jax.ShapeDtypeStruct(ocean_state.shape, f32),
        in_specs=[anywhere] * 7,
        out_specs=pl.BlockSpec(memory_space=pltpu.VMEM),
        scratch_shapes=[
            pltpu.VMEM(ocean_state.shape, f32),
            pltpu.VMEM((rows, lanes), jnp.int32),
            pltpu.VMEM(tile, f32),
            pltpu.VMEM((blocks, fields, cells), jnp.bfloat16),
            pltpu.VMEM((blocks, cells, lanes), jnp.bfloat16),
            pltpu.VMEM((1, blocks), jnp.int32),
            pltpu.VMEM((1, blocks), jnp.int32),
            pltpu.VMEM((2, levels * fields * rows + 2 * rows, lanes), f32),
            pltpu.VMEM(lat_shape, f32),
            pltpu.VMEM(row_shape, f32),
            pltpu.VMEM(row_shape, f32),
            pltpu.VMEM(row_shape, f32),
            pltpu.VMEM(row_shape, f32),
            pltpu.VMEM(lat_shape, f32),
            pltpu.VMEM(lat_shape, f32),
            pltpu.VMEM((fields, rows, lanes), f32),
            pltpu.VMEM((blocks, fields, lanes), f32),
            pltpu.VMEM((n_lon, MSG, lanes), f32),
            pltpu.VMEM((n_lon, MSG, lanes), f32),
            pltpu.VMEM((fields, rows, lanes), f32),
        ]
        + [pltpu.VMEM(tile, f32)] * 7
        + [
            pltpu.VMEM((levels, fields, rows, lanes), f32),
            pltpu.SemaphoreType.DMA((1 + CHUNKS + 5,)),
            pltpu.SemaphoreType.DMA((2, CHUNKS, 4)),
            pltpu.SemaphoreType.DMA((2, CHUNKS, 4)),
            pltpu.SemaphoreType.DMA((2,)),
        ],
        compiler_params=pltpu.CompilerParams(
            collective_id=0, has_side_effects=True, vmem_limit_bytes=40 << 20
        ),
        cost_estimate=pl.CostEstimate(flops=20_000_000, bytes_accessed=5_200_000, transcendentals=0),
    )(*(pltpu.with_memory_space_constraint(x, pltpu.HBM) for x in (
        ocean_state, level_count, mix_rate, atmos_flux[0], remap_weight[0], remap_target, remap_slot
    )))


def solution(mesh):
    placed = (
        P(None, None, "lon", ("lat", "comp")),
        P("lon", ("lat", "comp")),
        P(None, "lon", ("lat", "comp")),
        P(("lat", "comp"), "lon", None, None),
        P(("lat", "comp"), "lon", None, None),
        P(("lat", "comp"), "lon"),
        P(("lat", "comp"), "lon"),
    )
    return jax.shard_map(
        local,
        mesh=mesh,
        in_specs=placed,
        out_specs=P(None, None, "lon", ("lat", "comp")),
        check_vma=False,
    )
```

```python
import functools

import jax
import jax.numpy as jnp
from jax import lax
from jax.experimental import pallas as pl
from jax.experimental.pallas import tpu as pltpu
from jax.sharding import PartitionSpec as P

DIFFUSE = 0.2
ADVECTION = 0.5
THERMAL = 0.2
HALINE = 0.15
GRAVITY = 0.05
CORIOLIS = 0.3
SURFACE_GAIN = (0.5, 0.4, 0.6, 0.6)

FIELDS = 4
ROWS = 8
LANES = 128
CHUNKS = 4
UNROLL = 10
PIECES = 4
MSG = FIELDS + 1
MESH = pl.DeviceIdType.MESH


def window(
    n_lon, n_lat, n_comp, levels,
    state, count, rate, flux, weight, target, slot, val, bt_ref,
    raw, cnt, rt, fx, wt, tg, sl,
    grid_q, north_send, row_e, row_w, halo_e, halo_w, halo_n, halo_s, merged,
    part, outbox, inbox, force,
    c0_ref, ib_ref, ab_ref, bb_ref, it_ref, at_ref,
    in_sem, halo_send_sem, halo_recv_sem, msg_sem,
):
    per = levels // CHUNKS
    me = lax.axis_index("lon")
    depth = lax.axis_index("lat") * n_comp + lax.axis_index("comp")
    total = n_lat * n_comp
    east = lax.rem(me + 1, n_lon)
    west = lax.rem(me + n_lon - 1, n_lon)
    north = jnp.minimum(depth + 1, total - 1)
    south = jnp.maximum(depth - 1, 0)

    def lon_id(where):
        return {"lon": where}

    def lat_id(where):
        return {"lat": where // n_comp, "comp": lax.rem(where, n_comp)}

    barrier = pltpu.get_barrier_semaphore()
    has_north, has_south = depth < total - 1, depth > 0

    @pl.when(has_north)
    def _():
        pl.semaphore_signal(barrier, inc=1, device_id=lat_id(north), device_id_type=MESH)

    @pl.when(has_south)
    def _():
        pl.semaphore_signal(barrier, inc=1, device_id=lat_id(south), device_id_type=MESH)

    def greet(d, carry):
        pl.semaphore_signal(
            barrier, inc=1, device_id=lon_id(lax.rem(me + d, n_lon)), device_id_type=MESH
        )
        return carry

    lax.fori_loop(1, n_lon, greet, 0)

    @pl.when(jnp.logical_not(has_north))
    def _():
        halo_n[...] = jnp.zeros_like(halo_n)

    @pl.when(jnp.logical_not(has_south))
    def _():
        halo_s[...] = jnp.zeros_like(halo_s)

    cnt_in = pltpu.make_async_copy(count, cnt, in_sem.at[0])
    cnt_in.start()
    raw_in = []
    for c in range(CHUNKS):
        copy = pltpu.make_async_copy(
            state.at[:, pl.ds(c * per, per)], raw.at[:, pl.ds(c * per, per)], in_sem.at[1 + c]
        )
        copy.start()
        raw_in.append(copy)
    lane = lax.broadcasted_iota(jnp.int32, (ROWS, LANES), 1)
    row = lax.broadcasted_iota(jnp.int32, (ROWS, LANES), 0)
    first_lane, last_lane = lane == 0, lane == LANES - 1
    first_row, last_row = row == 0, row == ROWS - 1
    lane_half = lane // 2
    zero = jnp.zeros((ROWS, LANES), jnp.float32)

    def halo_copies(step, c):
        lo = ROWS + c * FIELDS * per
        size = FIELDS * per
        if step == 0 and c == 0:
            lo, size = 0, size + ROWS
        rows = pl.ds(lo, size)
        made = []
        for i, (src, dst, where) in enumerate((
            (row_e.at[step, rows], halo_w.at[step, rows], lon_id(east)),
            (row_w.at[step, rows], halo_e.at[step, rows], lon_id(west)),
            (north_send.at[step, c], halo_s.at[step, c], lat_id(north)),
            (north_send.at[step, c], halo_n.at[step, c], lat_id(south)),
        )):
            made.append(pltpu.make_async_remote_copy(
                src_ref=src,
                dst_ref=dst,
                send_sem=halo_send_sem.at[step, c, i],
                recv_sem=halo_recv_sem.at[step, c, i],
                device_id=where,
                device_id_type=MESH,
            ))
        return made

    def on_sides(made, act):
        act(made[0])
        act(made[1])

        @pl.when(has_north)
        def _():
            act(made[2])

        @pl.when(has_south)
        def _():
            act(made[3])

    def send_halos(step, c):
        on_sides(halo_copies(step, c), lambda copy: copy.start())

    def pack(step, c, kk, fields, packed):
        at = ROWS + (c * per + kk) * FIELDS
        made = []
        for f in range(FIELDS):
            q = fields[f]
            base = ROWS + ((c * per + kk) * FIELDS + f) * ROWS
            grid_q[step, pl.ds(pl.multiple_of(base, ROWS), ROWS), :] = q
            row_w[step, pl.ds(at + f, 1), :] = q[0:1, :]
            row_e[step, pl.ds(at + f, 1), :] = q[ROWS - 1:ROWS, :]
            turned = pltpu.roll(q, 2 * kk + 1, 1)
            made.append(jnp.where(lane_half == kk, turned, packed[f]))
        return tuple(made)

    cnt_in.wait()
    wet_count = cnt[...]
    wet_count_f = wet_count.astype(jnp.float32)
    for step in range(2):
        grid_q[step, pl.ds(0, ROWS), :] = zero
        grid_q[step, pl.ds(ROWS + levels * FIELDS * ROWS, ROWS), :] = zero
    row_w[0, pl.ds(0, ROWS), :] = jnp.broadcast_to(wet_count_f[0:1, :], (ROWS, LANES))
    row_e[0, pl.ds(0, ROWS), :] = jnp.broadcast_to(wet_count_f[ROWS - 1:, :], (ROWS, LANES))
    for c in range(CHUNKS):
        raw_in[c].wait()
        if c == 0:
            rest_in = []
            for i, (a, b) in enumerate(((target, tg), (slot, sl), (flux, fx), (weight, wt), (rate, rt))):
                copy = pltpu.make_async_copy(a, b, in_sem.at[1 + CHUNKS + i])
                copy.start()
                rest_in.append(copy)


        def pack_raw(kk, packed):
            k = c * per + kk
            wet = k < wet_count
            fields = [jnp.where(wet, raw[f, k], zero) for f in range(FIELDS)]
            return pack(0, c, kk, fields, packed)

        packed = lax.fori_loop(0, per, pack_raw, (zero,) * FIELDS, unroll=UNROLL)
        for f in range(FIELDS):
            tile = packed[f]
            if c == 0 and f == 0:
                turned = pltpu.roll(wet_count_f, 2 * per + 1, 1)
                tile = jnp.where(lane_half == per, turned, tile)
            north_send[0, c, f] = tile
        if c == 0:
            met = n_lon - 1 + has_north.astype(jnp.int32) + has_south.astype(jnp.int32)
            pl.semaphore_wait(barrier, met)
        send_halos(0, c)

    rest_in[0].wait()
    rest_in[1].wait()
    rest_in[2].wait()
    rest_in[3].wait()

    def one_block(b, carry):
        part[b] = jnp.dot(fx[b], wt[b], preferred_element_type=jnp.float32)
        return carry

    lax.fori_loop(0, n_lon, one_block, 0, unroll=UNROLL)
    chosen = (
        lax.broadcasted_iota(jnp.int32, (n_lon, n_lon), 0)
        == jnp.broadcast_to(tg[...], (n_lon, n_lon))
    )
    pick = jnp.where(chosen, 1.0, 0.0)
    slot_f = jnp.where(chosen, jnp.broadcast_to(sl[...].astype(jnp.float32), (n_lon, n_lon)), 0.0)
    half = jnp.bfloat16
    pick3 = jnp.concatenate([pick, pick, pick], axis=1).astype(half)
    for f in range(FIELDS):
        whole = part[:, f, :]
        high = whole.astype(half)
        rest = whole - high.astype(jnp.float32)
        middle = rest.astype(half)
        low = (rest - middle.astype(jnp.float32)).astype(half)
        outbox[:, f, :] = jnp.dot(
            pick3, jnp.concatenate([high, middle, low], axis=0),
            preferred_element_type=jnp.float32,
        )
    outbox[:, FIELDS, :] = jnp.broadcast_to(
        jnp.sum(slot_f, axis=1, keepdims=True), (n_lon, LANES)
    )

    def post(d, carry):
        owner = lax.rem(me + d, n_lon)
        pltpu.make_async_remote_copy(
            src_ref=outbox.at[owner],
            dst_ref=inbox.at[me],
            send_sem=msg_sem.at[0],
            recv_sem=msg_sem.at[1],
            device_id=lon_id(owner),
            device_id_type=MESH,
        ).start()
        return carry

    lax.fori_loop(1, n_lon, post, 0)

    rest_in[4].wait()

    def across(k):
        return jnp.where(k + 1 < wet_count, rt[k], zero)

    def factor(i, carry):
        below, inv_b, above, inv_t = carry
        k = levels - 1 - i
        upper = across(jnp.maximum(k - 1, 0))
        upper = jnp.where(k > 0, upper, 0.0)
        inv_b = 1.0 / (1.0 + upper + below - below * below * inv_b)
        masked = jnp.where(k < wet_count, inv_b, 0.0)
        ib_ref[k] = masked
        ab_ref[k] = below * masked
        bb_ref[k] = jnp.where(k > 0, upper, 1.0) * masked
        lower = jnp.where(i < levels - 1, across(i), 0.0)
        inv_t = 1.0 / (1.0 + above + lower - above * above * inv_t)
        masked = jnp.where(i < wet_count, inv_t, 0.0)
        it_ref[i] = masked
        at_ref[i] = jnp.where(i > 0, above, 1.0) * masked
        bt_ref[i] = lower * masked
        return upper, inv_b, lower, inv_t

    lax.fori_loop(0, levels, factor, (zero,) * 4, unroll=UNROLL)

    odd = lax.rem(lane, 2) == 1

    def arrive(step, c):
        made = halo_copies(step, c)
        made[0].wait_recv()
        made[1].wait_recv()

        @pl.when(has_south)
        def _():
            made[2].wait_recv()

        @pl.when(has_north)
        def _():
            made[3].wait_recv()

        for f in range(FIELDS):
            merged[f] = jnp.where(odd, halo_n[step, c, f], halo_s[step, c, f])

    def lat_pair(q, tile, kk):
        edge = pltpu.roll(tile, LANES - 1 - 2 * kk, 1)
        n = pltpu.roll(jnp.where(first_lane, edge, q), LANES - 1, 1)
        s = pltpu.roll(jnp.where(last_lane, edge, q), 1, 1)
        return n, s

    def row_of(ref, step, at):
        return jnp.broadcast_to(ref[step, pl.ds(at, 1), :], (ROWS, LANES))

    y = (depth * LANES + lane).astype(jnp.float32)
    turning = CORIOLIS * (2.0 * (y + 0.5) / (total * LANES) - 1.0)

    def tendency(step, c, kk, sums, counts):
        k = c * per + kk
        at = ROWS + k * FIELDS
        mid, e, w, n, s = [], [], [], [], []
        for f in range(FIELDS):
            base = ROWS + (k * FIELDS + f) * ROWS
            q = grid_q[step, pl.ds(pl.multiple_of(base, ROWS), ROWS), :]
            e.append(jnp.where(last_row, row_of(halo_e, step, at + f), pltpu.roll(q, ROWS - 1, 0)))
            w.append(jnp.where(first_row, row_of(halo_w, step, at + f), pltpu.roll(q, 1, 0)))
            up, down = lat_pair(q, merged[f], kk)
            n.append(up)
            s.append(down)
            mid.append(q)
        wets = [k < a for a in counts]
        if step == 0:
            shares = [jnp.where(m, DIFFUSE, 0.0) for m in wets]
            c0 = (1.0 - (shares[0] + shares[1])) - (shares[2] + shares[3])
            c0_ref[k] = c0
        else:
            c0 = c0_ref[k]
        half = 0.5 * ADVECTION
        a, b = half * mid[2], half * mid[3]
        to_e, to_w, to_n, to_s = DIFFUSE - a, DIFFUSE + a, DIFFUSE - b, DIFFUSE + b
        new = []
        for f in range(2):
            new.append(
                c0 * mid[f]
                + ((to_e * e[f] + to_w * w[f]) + (to_n * n[f] + to_s * s[f]))
            )
        scale = 0.5 * GRAVITY
        made, pressures = [], []
        for side, m, total_d in zip((e, w, n, s), wets, sums):
            total_d = total_d + (scale * HALINE * side[1] - scale * THERMAL * side[0])
            made.append(total_d)
            pressures.append(jnp.where(m, total_d, 0.0))
        for f, sign, lo, hi in ((2, 1, 1, 0), (3, -1, 3, 2)):
            spread = DIFFUSE * ((e[f] + w[f]) + (n[f] + s[f]))
            twist = turning * mid[5 - f]
            base = c0 * mid[f] + spread
            base = base + twist if sign > 0 else base - twist
            new.append(base - (pressures[hi] - pressures[lo]))
        return new, tuple(made)

    arrive(0, 0)
    count_e = jnp.where(last_row, halo_e[0, pl.ds(0, ROWS), :], pltpu.roll(wet_count_f, ROWS - 1, 0))
    count_w = jnp.where(first_row, halo_w[0, pl.ds(0, ROWS), :], pltpu.roll(wet_count_f, 1, 0))
    count_n, count_s = lat_pair(wet_count_f, merged[0], per)
    counts = [a.astype(jnp.int32) for a in (count_e, count_w, count_n, count_s)]
    sums = (zero,) * 4
    for c in range(CHUNKS):
        if c > 0:
            arrive(0, c)

        def first(kk, sums):
            new, sums = tendency(0, c, kk, sums, counts)
            k = c * per + kk
            ib = ib_ref[k]
            for f in range(FIELDS):
                val[k, f] = ib * new[f]
            return sums

        sums = lax.fori_loop(0, per, first, sums, unroll=UNROLL)

    def upward(i, carry):
        k = levels - 1 - i
        ab = ab_ref[k]
        made = tuple(val[k, f] + ab * carry[f] for f in range(FIELDS))
        for f in range(FIELDS):
            val[k, f] = made[f]
        return made

    lax.fori_loop(0, levels, upward, (zero,) * FIELDS, unroll=UNROLL)

    inbox[me] = outbox[me]
    pltpu.make_async_copy(
        inbox.at[pl.ds(0, n_lon - 1)], inbox.at[pl.ds(0, n_lon - 1)], msg_sem.at[1]
    ).wait()
    row_f = row.astype(jnp.float32)

    def receive(s, carry):
        hit = row_f == jnp.broadcast_to(inbox[s, pl.ds(FIELDS, 1), :], (ROWS, LANES))
        return tuple(
            carry[f]
            + jnp.where(hit, jnp.broadcast_to(inbox[s, pl.ds(f, 1), :], (ROWS, LANES)), 0.0)
            for f in range(FIELDS)
        )

    forced = lax.fori_loop(0, n_lon, receive, (zero,) * FIELDS, unroll=UNROLL)
    for f in range(FIELDS):
        force[f] = SURFACE_GAIN[f] * forced[f]

    carry = tuple(force[f] for f in range(FIELDS))
    for c in range(CHUNKS):

        def downward(kk, carry):
            before, packed = carry
            k = c * per + kk
            bb = bb_ref[k]
            made = tuple(val[k, f] + bb * before[f] for f in range(FIELDS))
            return made, pack(1, c, kk, made, packed)

        carry, packed = lax.fori_loop(0, per, downward, (carry, (zero,) * FIELDS), unroll=UNROLL)
        for f in range(FIELDS):
            north_send[1, c, f] = packed[f]
        send_halos(1, c)

    sums = (zero,) * 4
    carry = tuple(force[f] for f in range(FIELDS))
    for c in range(CHUNKS):
        arrive(1, c)

        def second(kk, state_in):
            sums, before = state_in
            new, sums = tendency(1, c, kk, sums, counts)
            k = c * per + kk
            it, at = it_ref[k], at_ref[k]
            made = tuple(it * new[f] + at * before[f] for f in range(FIELDS))
            for f in range(FIELDS):
                val[k, f] = made[f]
            return sums, made

        sums, carry = lax.fori_loop(0, per, second, (sums, carry), unroll=UNROLL)

    for step in range(2):
        for c in range(CHUNKS):
            on_sides(halo_copies(step, c), lambda copy: copy.wait_send())
    pltpu.make_async_copy(
        outbox.at[pl.ds(0, n_lon - 1)], outbox.at[pl.ds(0, n_lon - 1)], msg_sem.at[0]
    ).wait()


def finish(levels, val, bt_ref, out, res, sem):
    per = levels // PIECES
    carry = (jnp.zeros((ROWS, LANES), jnp.float32),) * FIELDS
    outs = []
    for c in reversed(range(PIECES)):

        def settle(i, carry):
            k = c * per + per - 1 - i
            bt = bt_ref[k]
            made = tuple(val[k, f] + bt * carry[f] for f in range(FIELDS))
            for f in range(FIELDS):
                res[f, k] = made[f]
            return made

        carry = lax.fori_loop(0, per, settle, carry, unroll=10)
        here = pl.ds(c * per, per)
        copy = pltpu.make_async_copy(res.at[:, here], out.at[:, here], sem.at[c])
        copy.start()
        outs.append(copy)
    for copy in outs:
        copy.wait()


def local(ocean_state, level_count, mix_rate, atmos_flux, remap_weight, remap_target, remap_slot):
    fields, levels, rows, lanes = ocean_state.shape
    n_lon, n_lat, n_comp = (lax.axis_size(a) for a in ("lon", "lat", "comp"))
    blocks, cells = atmos_flux.shape[1], atmos_flux.shape[3]
    per = levels // CHUNKS
    tile = (levels, rows, lanes)
    f32 = jnp.float32
    row_shape = (2, ROWS + levels * fields, lanes)
    lat_shape = (2, CHUNKS, fields, rows, lanes)
    anywhere = pl.BlockSpec(memory_space=pltpu.HBM)
    inside = pl.BlockSpec(memory_space=pltpu.VMEM)
    stack = (levels, fields, rows, lanes)
    val, bt = pl.pallas_call(
        functools.partial(window, n_lon, n_lat, n_comp, levels),
        out_shape=(jax.ShapeDtypeStruct(stack, f32), jax.ShapeDtypeStruct(tile, f32)),
        in_specs=[anywhere] * 7,
        out_specs=(inside, inside),
        scratch_shapes=[
            pltpu.VMEM(ocean_state.shape, f32),
            pltpu.VMEM((rows, lanes), jnp.int32),
            pltpu.VMEM(tile, f32),
            pltpu.VMEM((blocks, fields, cells), jnp.bfloat16),
            pltpu.VMEM((blocks, cells, lanes), jnp.bfloat16),
            pltpu.VMEM((1, blocks), jnp.int32),
            pltpu.VMEM((1, blocks), jnp.int32),
            pltpu.VMEM((2, levels * fields * rows + 2 * rows, lanes), f32),
            pltpu.VMEM(lat_shape, f32),
            pltpu.VMEM(row_shape, f32),
            pltpu.VMEM(row_shape, f32),
            pltpu.VMEM(row_shape, f32),
            pltpu.VMEM(row_shape, f32),
            pltpu.VMEM(lat_shape, f32),
            pltpu.VMEM(lat_shape, f32),
            pltpu.VMEM((fields, rows, lanes), f32),
            pltpu.VMEM((blocks, fields, lanes), f32),
            pltpu.VMEM((n_lon, MSG, lanes), f32),
            pltpu.VMEM((n_lon, MSG, lanes), f32),
            pltpu.VMEM((fields, rows, lanes), f32),
        ]
        + [pltpu.VMEM(tile, f32)] * 6
        + [
            pltpu.SemaphoreType.DMA((1 + CHUNKS + 5,)),
            pltpu.SemaphoreType.DMA((2, CHUNKS, 4)),
            pltpu.SemaphoreType.DMA((2, CHUNKS, 4)),
            pltpu.SemaphoreType.DMA((2,)),
        ],
        compiler_params=pltpu.CompilerParams(
            collective_id=0, has_side_effects=True, vmem_limit_bytes=40 << 20
        ),
        cost_estimate=pl.CostEstimate(flops=20_000_000, bytes_accessed=5_200_000, transcendentals=0),
    )(*(pltpu.with_memory_space_constraint(x, pltpu.HBM) for x in (
        ocean_state, level_count, mix_rate, atmos_flux[0], remap_weight[0], remap_target, remap_slot
    )))

    return pl.pallas_call(
        functools.partial(finish, levels),
        out_shape=jax.ShapeDtypeStruct(ocean_state.shape, f32),
        in_specs=[inside, inside],
        out_specs=anywhere,
        scratch_shapes=[
            pltpu.VMEM(ocean_state.shape, f32),
            pltpu.SemaphoreType.DMA((PIECES,)),
        ],
        compiler_params=pltpu.CompilerParams(vmem_limit_bytes=16 << 20),
        cost_estimate=pl.CostEstimate(flops=700_000, bytes_accessed=3_000_000, transcendentals=0),
    )(val, bt)


def solution(mesh):
    placed = (
        P(None, None, "lon", ("lat", "comp")),
        P("lon", ("lat", "comp")),
        P(None, "lon", ("lat", "comp")),
        P(("lat", "comp"), "lon", None, None),
        P(("lat", "comp"), "lon", None, None),
        P(("lat", "comp"), "lon"),
        P(("lat", "comp"), "lon"),
    )
    return jax.shard_map(
        local,
        mesh=mesh,
        in_specs=placed,
        out_specs=P(None, None, "lon", ("lat", "comp")),
        check_vma=False,
    )
```

```python
import functools

import jax
import jax.numpy as jnp
from jax import lax
from jax.experimental import pallas as pl
from jax.experimental.pallas import tpu as pltpu
from jax.sharding import PartitionSpec as P

DIFFUSE = 0.2
ADVECTION = 0.5
THERMAL = 0.2
HALINE = 0.15
GRAVITY = 0.05
CORIOLIS = 0.3
SURFACE_GAIN = (0.5, 0.4, 0.6, 0.6)

FIELDS = 4
ROWS = 8
LANES = 128
CHUNKS = 4
UNROLL = 10
PIECES = 4
ROW = 8
MSG = FIELDS + 1
MESH = pl.DeviceIdType.MESH


def window(
    n_lon, n_lat, n_comp, levels,
    state, count, rate, flux, weight, target, slot, val, bt_ref,
    raw, cnt, rt, fx, wt, tg, sl,
    grid_q, north_send, row_e, row_w, halo_e, halo_w, halo_n, halo_s, merged,
    part, outbox, inbox, force,
    c0_ref, ib_ref, ab_ref, bb_ref, it_ref, at_ref,
    in_sem, halo_send_sem, halo_recv_sem, msg_sem, column_sem,
):
    per = levels // CHUNKS
    me = lax.axis_index("lon")
    depth = lax.axis_index("lat") * n_comp + lax.axis_index("comp")
    total = n_lat * n_comp
    east = lax.rem(me + 1, n_lon)
    west = lax.rem(me + n_lon - 1, n_lon)
    north = jnp.minimum(depth + 1, total - 1)
    south = jnp.maximum(depth - 1, 0)

    def lon_id(where):
        return {"lon": where}

    def lat_id(where):
        return {"lat": where // n_comp, "comp": lax.rem(where, n_comp)}

    barrier = pltpu.get_barrier_semaphore()
    has_north, has_south = depth < total - 1, depth > 0

    @pl.when(has_north)
    def _():
        pl.semaphore_signal(barrier, inc=1, device_id=lat_id(north), device_id_type=MESH)

    @pl.when(has_south)
    def _():
        pl.semaphore_signal(barrier, inc=1, device_id=lat_id(south), device_id_type=MESH)

    wide = min(ROW, n_lon)
    tall = n_lon // wide
    place = lax.rem(me, wide)
    base = me - place

    def greet(sem, where):
        pl.semaphore_signal(sem, inc=1, device_id=lon_id(where), device_id_type=MESH)

    def greet_row(sem):
        def one(d, carry):
            greet(sem, base + lax.rem(place + d, wide))
            return carry

        lax.fori_loop(1, wide, one, 0)

    ends_row, starts_row = place == wide - 1, place == 0
    if tall > 1:

        @pl.when(ends_row)
        def _():
            greet(barrier, east)

        @pl.when(starts_row)
        def _():
            greet(barrier, west)

        for d in range(1, tall):
            greet(barrier, lax.rem(me + d * wide, n_lon))
    greet_row(barrier)

    @pl.when(jnp.logical_not(has_north))
    def _():
        halo_n[...] = jnp.zeros_like(halo_n)

    @pl.when(jnp.logical_not(has_south))
    def _():
        halo_s[...] = jnp.zeros_like(halo_s)

    cnt_in = pltpu.make_async_copy(count, cnt, in_sem.at[0])
    cnt_in.start()
    raw_in = []
    for c in range(CHUNKS):
        copy = pltpu.make_async_copy(
            state.at[:, pl.ds(c * per, per)], raw.at[:, pl.ds(c * per, per)], in_sem.at[1 + c]
        )
        copy.start()
        raw_in.append(copy)
    lane = lax.broadcasted_iota(jnp.int32, (ROWS, LANES), 1)
    row = lax.broadcasted_iota(jnp.int32, (ROWS, LANES), 0)
    first_lane, last_lane = lane == 0, lane == LANES - 1
    first_row, last_row = row == 0, row == ROWS - 1
    lane_half = lane // 2
    zero = jnp.zeros((ROWS, LANES), jnp.float32)

    def halo_copies(step, c):
        lo = ROWS + c * FIELDS * per
        size = FIELDS * per
        if step == 0 and c == 0:
            lo, size = 0, size + ROWS
        rows = pl.ds(lo, size)
        made = []
        for i, (src, dst, where) in enumerate((
            (row_e.at[step, rows], halo_w.at[step, rows], lon_id(east)),
            (row_w.at[step, rows], halo_e.at[step, rows], lon_id(west)),
            (north_send.at[step, c], halo_s.at[step, c], lat_id(north)),
            (north_send.at[step, c], halo_n.at[step, c], lat_id(south)),
        )):
            made.append(pltpu.make_async_remote_copy(
                src_ref=src,
                dst_ref=dst,
                send_sem=halo_send_sem.at[step, c, i],
                recv_sem=halo_recv_sem.at[step, c, i],
                device_id=where,
                device_id_type=MESH,
            ))
        return made

    def on_sides(made, act):
        act(made[0])
        act(made[1])

        @pl.when(has_north)
        def _():
            act(made[2])

        @pl.when(has_south)
        def _():
            act(made[3])

    def send_halos(step, c):
        on_sides(halo_copies(step, c), lambda copy: copy.start())

    def pack(step, c, kk, fields, packed):
        at = ROWS + (c * per + kk) * FIELDS
        made = []
        for f in range(FIELDS):
            q = fields[f]
            base = ROWS + ((c * per + kk) * FIELDS + f) * ROWS
            grid_q[step, pl.ds(pl.multiple_of(base, ROWS), ROWS), :] = q
            row_w[step, pl.ds(at + f, 1), :] = q[0:1, :]
            row_e[step, pl.ds(at + f, 1), :] = q[ROWS - 1:ROWS, :]
            turned = pltpu.roll(q, 2 * kk + 1, 1)
            made.append(jnp.where(lane_half == kk, turned, packed[f]))
        return tuple(made)

    cnt_in.wait()
    wet_count = cnt[...]
    wet_count_f = wet_count.astype(jnp.float32)
    for step in range(2):
        grid_q[step, pl.ds(0, ROWS), :] = zero
        grid_q[step, pl.ds(ROWS + levels * FIELDS * ROWS, ROWS), :] = zero
    row_w[0, pl.ds(0, ROWS), :] = jnp.broadcast_to(wet_count_f[0:1, :], (ROWS, LANES))
    row_e[0, pl.ds(0, ROWS), :] = jnp.broadcast_to(wet_count_f[ROWS - 1:, :], (ROWS, LANES))
    for c in range(CHUNKS):
        raw_in[c].wait()
        if c == 0:
            rest_in = []
            for i, (a, b) in enumerate(((target, tg), (slot, sl), (flux, fx), (weight, wt), (rate, rt))):
                copy = pltpu.make_async_copy(a, b, in_sem.at[1 + CHUNKS + i])
                copy.start()
                rest_in.append(copy)


        def pack_raw(kk, packed):
            k = c * per + kk
            wet = k < wet_count
            fields = [jnp.where(wet, raw[f, k], zero) for f in range(FIELDS)]
            return pack(0, c, kk, fields, packed)

        packed = lax.fori_loop(0, per, pack_raw, (zero,) * FIELDS, unroll=UNROLL)
        for f in range(FIELDS):
            tile = packed[f]
            if c == 0 and f == 0:
                turned = pltpu.roll(wet_count_f, 2 * per + 1, 1)
                tile = jnp.where(lane_half == per, turned, tile)
            north_send[0, c, f] = tile
        if c == 0:
            met = wide - 1 + has_north.astype(jnp.int32) + has_south.astype(jnp.int32)
            if tall > 1:
                met = met + tall - 1 + ends_row.astype(jnp.int32) + starts_row.astype(jnp.int32)
            pl.semaphore_wait(barrier, met)
            greet_row(column_sem)
        send_halos(0, c)

    rest_in[0].wait()
    rest_in[1].wait()
    rest_in[2].wait()
    rest_in[3].wait()

    def one_block(b, carry):
        part[b] = jnp.dot(fx[b], wt[b], preferred_element_type=jnp.float32)
        return carry

    lax.fori_loop(0, n_lon, one_block, 0, unroll=UNROLL)
    chosen = (
        lax.broadcasted_iota(jnp.int32, (n_lon, n_lon), 0)
        == jnp.broadcast_to(tg[...], (n_lon, n_lon))
    )
    pick = jnp.where(chosen, 1.0, 0.0)
    slot_f = jnp.where(chosen, jnp.broadcast_to(sl[...].astype(jnp.float32), (n_lon, n_lon)), 0.0)
    half = jnp.bfloat16
    pick3 = jnp.concatenate([pick, pick, pick], axis=1).astype(half)
    for f in range(FIELDS):
        whole = part[:, f, :]
        high = whole.astype(half)
        rest = whole - high.astype(jnp.float32)
        middle = rest.astype(half)
        low = (rest - middle.astype(jnp.float32)).astype(half)
        outbox[:, f, :] = jnp.dot(
            pick3, jnp.concatenate([high, middle, low], axis=0),
            preferred_element_type=jnp.float32,
        )
    outbox[:, FIELDS, :] = jnp.broadcast_to(
        jnp.sum(slot_f, axis=1, keepdims=True), (n_lon, LANES)
    )

    def post(d, carry):
        owner = lax.rem(me + d, n_lon)
        pltpu.make_async_remote_copy(
            src_ref=outbox.at[owner],
            dst_ref=inbox.at[me],
            send_sem=msg_sem.at[0],
            recv_sem=msg_sem.at[1],
            device_id=lon_id(owner),
            device_id_type=MESH,
        ).start()
        return carry

    pl.semaphore_wait(column_sem, wide - 1)
    lax.fori_loop(1, n_lon, post, 0)

    rest_in[4].wait()

    def across(k):
        return jnp.where(k + 1 < wet_count, rt[k], zero)

    def factor(i, carry):
        below, inv_b, above, inv_t = carry
        k = levels - 1 - i
        upper = across(jnp.maximum(k - 1, 0))
        upper = jnp.where(k > 0, upper, 0.0)
        inv_b = 1.0 / (1.0 + upper + below - below * below * inv_b)
        masked = jnp.where(k < wet_count, inv_b, 0.0)
        ib_ref[k] = masked
        ab_ref[k] = below * masked
        bb_ref[k] = jnp.where(k > 0, upper, 1.0) * masked
        lower = jnp.where(i < levels - 1, across(i), 0.0)
        inv_t = 1.0 / (1.0 + above + lower - above * above * inv_t)
        masked = jnp.where(i < wet_count, inv_t, 0.0)
        it_ref[i] = masked
        at_ref[i] = jnp.where(i > 0, above, 1.0) * masked
        bt_ref[i] = lower * masked
        return upper, inv_b, lower, inv_t

    lax.fori_loop(0, levels, factor, (zero,) * 4, unroll=UNROLL)

    odd = lax.rem(lane, 2) == 1

    def arrive(step, c):
        made = halo_copies(step, c)
        made[0].wait_recv()
        made[1].wait_recv()

        @pl.when(has_south)
        def _():
            made[2].wait_recv()

        @pl.when(has_north)
        def _():
            made[3].wait_recv()

        for f in range(FIELDS):
            merged[f] = jnp.where(odd, halo_n[step, c, f], halo_s[step, c, f])

    def lat_pair(q, tile, kk):
        edge = pltpu.roll(tile, LANES - 1 - 2 * kk, 1)
        n = pltpu.roll(jnp.where(first_lane, edge, q), LANES - 1, 1)
        s = pltpu.roll(jnp.where(last_lane, edge, q), 1, 1)
        return n, s

    def row_of(ref, step, at):
        return jnp.broadcast_to(ref[step, pl.ds(at, 1), :], (ROWS, LANES))

    y = (depth * LANES + lane).astype(jnp.float32)
    turning = CORIOLIS * (2.0 * (y + 0.5) / (total * LANES) - 1.0)

    def tendency(step, c, kk, sums, counts):
        k = c * per + kk
        at = ROWS + k * FIELDS
        mid, e, w, n, s = [], [], [], [], []
        for f in range(FIELDS):
            base = ROWS + (k * FIELDS + f) * ROWS
            q = grid_q[step, pl.ds(pl.multiple_of(base, ROWS), ROWS), :]
            e.append(jnp.where(last_row, row_of(halo_e, step, at + f), pltpu.roll(q, ROWS - 1, 0)))
            w.append(jnp.where(first_row, row_of(halo_w, step, at + f), pltpu.roll(q, 1, 0)))
            up, down = lat_pair(q, merged[f], kk)
            n.append(up)
            s.append(down)
            mid.append(q)
        wets = [k < a for a in counts]
        if step == 0:
            shares = [jnp.where(m, DIFFUSE, 0.0) for m in wets]
            c0 = (1.0 - (shares[0] + shares[1])) - (shares[2] + shares[3])
            c0_ref[k] = c0
        else:
            c0 = c0_ref[k]
        half = 0.5 * ADVECTION
        a, b = half * mid[2], half * mid[3]
        to_e, to_w, to_n, to_s = DIFFUSE - a, DIFFUSE + a, DIFFUSE - b, DIFFUSE + b
        new = []
        for f in range(2):
            new.append(
                c0 * mid[f]
                + ((to_e * e[f] + to_w * w[f]) + (to_n * n[f] + to_s * s[f]))
            )
        scale = 0.5 * GRAVITY
        made, pressures = [], []
        for side, m, total_d in zip((e, w, n, s), wets, sums):
            total_d = total_d + (scale * HALINE * side[1] - scale * THERMAL * side[0])
            made.append(total_d)
            pressures.append(jnp.where(m, total_d, 0.0))
        for f, sign, lo, hi in ((2, 1, 1, 0), (3, -1, 3, 2)):
            spread = DIFFUSE * ((e[f] + w[f]) + (n[f] + s[f]))
            twist = turning * mid[5 - f]
            base = c0 * mid[f] + spread
            base = base + twist if sign > 0 else base - twist
            new.append(base - (pressures[hi] - pressures[lo]))
        return new, tuple(made)

    arrive(0, 0)
    count_e = jnp.where(last_row, halo_e[0, pl.ds(0, ROWS), :], pltpu.roll(wet_count_f, ROWS - 1, 0))
    count_w = jnp.where(first_row, halo_w[0, pl.ds(0, ROWS), :], pltpu.roll(wet_count_f, 1, 0))
    count_n, count_s = lat_pair(wet_count_f, merged[0], per)
    counts = [a.astype(jnp.int32) for a in (count_e, count_w, count_n, count_s)]
    sums = (zero,) * 4
    for c in range(CHUNKS):
        if c > 0:
            arrive(0, c)

        def first(kk, sums):
            new, sums = tendency(0, c, kk, sums, counts)
            k = c * per + kk
            ib = ib_ref[k]
            for f in range(FIELDS):
                val[k, f] = ib * new[f]
            return sums

        sums = lax.fori_loop(0, per, first, sums, unroll=UNROLL)

    def upward(i, carry):
        k = levels - 1 - i
        ab = ab_ref[k]
        made = tuple(val[k, f] + ab * carry[f] for f in range(FIELDS))
        for f in range(FIELDS):
            val[k, f] = made[f]
        return made

    lax.fori_loop(0, levels, upward, (zero,) * FIELDS, unroll=UNROLL)

    inbox[me] = outbox[me]
    pltpu.make_async_copy(
        inbox.at[pl.ds(0, n_lon - 1)], inbox.at[pl.ds(0, n_lon - 1)], msg_sem.at[1]
    ).wait()
    row_f = row.astype(jnp.float32)

    def receive(s, carry):
        hit = row_f == jnp.broadcast_to(inbox[s, pl.ds(FIELDS, 1), :], (ROWS, LANES))
        return tuple(
            carry[f]
            + jnp.where(hit, jnp.broadcast_to(inbox[s, pl.ds(f, 1), :], (ROWS, LANES)), 0.0)
            for f in range(FIELDS)
        )

    forced = lax.fori_loop(0, n_lon, receive, (zero,) * FIELDS, unroll=UNROLL)
    for f in range(FIELDS):
        force[f] = SURFACE_GAIN[f] * forced[f]

    carry = tuple(force[f] for f in range(FIELDS))
    for c in range(CHUNKS):

        def downward(kk, carry):
            before, packed = carry
            k = c * per + kk
            bb = bb_ref[k]
            made = tuple(val[k, f] + bb * before[f] for f in range(FIELDS))
            return made, pack(1, c, kk, made, packed)

        carry, packed = lax.fori_loop(0, per, downward, (carry, (zero,) * FIELDS), unroll=UNROLL)
        for f in range(FIELDS):
            north_send[1, c, f] = packed[f]
        send_halos(1, c)

    sums = (zero,) * 4
    carry = tuple(force[f] for f in range(FIELDS))
    for c in range(CHUNKS):
        arrive(1, c)

        def second(kk, state_in):
            sums, before = state_in
            new, sums = tendency(1, c, kk, sums, counts)
            k = c * per + kk
            it, at = it_ref[k], at_ref[k]
            made = tuple(it * new[f] + at * before[f] for f in range(FIELDS))
            for f in range(FIELDS):
                val[k, f] = made[f]
            return sums, made

        sums, carry = lax.fori_loop(0, per, second, (sums, carry), unroll=UNROLL)

    for step in range(2):
        for c in range(CHUNKS):
            on_sides(halo_copies(step, c), lambda copy: copy.wait_send())
    pltpu.make_async_copy(
        outbox.at[pl.ds(0, n_lon - 1)], outbox.at[pl.ds(0, n_lon - 1)], msg_sem.at[0]
    ).wait()


def finish(levels, val, bt_ref, out, res, sem):
    per = levels // PIECES
    carry = (jnp.zeros((ROWS, LANES), jnp.float32),) * FIELDS
    outs = []
    for c in reversed(range(PIECES)):

        def settle(i, carry):
            k = c * per + per - 1 - i
            bt = bt_ref[k]
            made = tuple(val[k, f] + bt * carry[f] for f in range(FIELDS))
            for f in range(FIELDS):
                res[f, k] = made[f]
            return made

        carry = lax.fori_loop(0, per, settle, carry, unroll=10)
        here = pl.ds(c * per, per)
        copy = pltpu.make_async_copy(res.at[:, here], out.at[:, here], sem.at[c])
        copy.start()
        outs.append(copy)
    for copy in outs:
        copy.wait()


def local(ocean_state, level_count, mix_rate, atmos_flux, remap_weight, remap_target, remap_slot):
    fields, levels, rows, lanes = ocean_state.shape
    n_lon, n_lat, n_comp = (lax.axis_size(a) for a in ("lon", "lat", "comp"))
    blocks, cells = atmos_flux.shape[1], atmos_flux.shape[3]
    per = levels // CHUNKS
    tile = (levels, rows, lanes)
    f32 = jnp.float32
    row_shape = (2, ROWS + levels * fields, lanes)
    lat_shape = (2, CHUNKS, fields, rows, lanes)
    anywhere = pl.BlockSpec(memory_space=pltpu.HBM)
    inside = pl.BlockSpec(memory_space=pltpu.VMEM)
    stack = (levels, fields, rows, lanes)
    val, bt = pl.pallas_call(
        functools.partial(window, n_lon, n_lat, n_comp, levels),
        out_shape=(jax.ShapeDtypeStruct(stack, f32), jax.ShapeDtypeStruct(tile, f32)),
        in_specs=[anywhere] * 7,
        out_specs=(inside, inside),
        scratch_shapes=[
            pltpu.VMEM(ocean_state.shape, f32),
            pltpu.VMEM((rows, lanes), jnp.int32),
            pltpu.VMEM(tile, f32),
            pltpu.VMEM((blocks, fields, cells), jnp.bfloat16),
            pltpu.VMEM((blocks, cells, lanes), jnp.bfloat16),
            pltpu.VMEM((1, blocks), jnp.int32),
            pltpu.VMEM((1, blocks), jnp.int32),
            pltpu.VMEM((2, levels * fields * rows + 2 * rows, lanes), f32),
            pltpu.VMEM(lat_shape, f32),
            pltpu.VMEM(row_shape, f32),
            pltpu.VMEM(row_shape, f32),
            pltpu.VMEM(row_shape, f32),
            pltpu.VMEM(row_shape, f32),
            pltpu.VMEM(lat_shape, f32),
            pltpu.VMEM(lat_shape, f32),
            pltpu.VMEM((fields, rows, lanes), f32),
            pltpu.VMEM((blocks, fields, lanes), f32),
            pltpu.VMEM((n_lon, MSG, lanes), f32),
            pltpu.VMEM((n_lon, MSG, lanes), f32),
            pltpu.VMEM((fields, rows, lanes), f32),
        ]
        + [pltpu.VMEM(tile, f32)] * 6
        + [
            pltpu.SemaphoreType.DMA((1 + CHUNKS + 5,)),
            pltpu.SemaphoreType.DMA((2, CHUNKS, 4)),
            pltpu.SemaphoreType.DMA((2, CHUNKS, 4)),
            pltpu.SemaphoreType.DMA((2,)),
            pltpu.SemaphoreType.REGULAR,
        ],
        compiler_params=pltpu.CompilerParams(
            collective_id=0, has_side_effects=True, vmem_limit_bytes=40 << 20
        ),
        cost_estimate=pl.CostEstimate(flops=20_000_000, bytes_accessed=5_200_000, transcendentals=0),
    )(*(pltpu.with_memory_space_constraint(x, pltpu.HBM) for x in (
        ocean_state, level_count, mix_rate, atmos_flux[0], remap_weight[0], remap_target, remap_slot
    )))

    return pl.pallas_call(
        functools.partial(finish, levels),
        out_shape=jax.ShapeDtypeStruct(ocean_state.shape, f32),
        in_specs=[inside, inside],
        out_specs=anywhere,
        scratch_shapes=[
            pltpu.VMEM(ocean_state.shape, f32),
            pltpu.SemaphoreType.DMA((PIECES,)),
        ],
        compiler_params=pltpu.CompilerParams(vmem_limit_bytes=16 << 20),
        cost_estimate=pl.CostEstimate(flops=700_000, bytes_accessed=3_000_000, transcendentals=0),
    )(val, bt)


def solution(mesh):
    placed = (
        P(None, None, "lon", ("lat", "comp")),
        P("lon", ("lat", "comp")),
        P(None, "lon", ("lat", "comp")),
        P(("lat", "comp"), "lon", None, None),
        P(("lat", "comp"), "lon", None, None),
        P(("lat", "comp"), "lon"),
        P(("lat", "comp"), "lon"),
    )
    return jax.shard_map(
        local,
        mesh=mesh,
        in_specs=placed,
        out_specs=P(None, None, "lon", ("lat", "comp")),
        check_vma=False,
    )
```

```python
import functools

import jax
import jax.numpy as jnp
from jax import lax
from jax.experimental import pallas as pl
from jax.experimental.pallas import tpu as pltpu
from jax.sharding import PartitionSpec as P

DIFFUSE = 0.2
ADVECTION = 0.5
THERMAL = 0.2
HALINE = 0.15
GRAVITY = 0.05
CORIOLIS = 0.3
SURFACE_GAIN = (0.5, 0.4, 0.6, 0.6)

FIELDS = 4
ROWS = 8
LANES = 128
CHUNKS = 4
UNROLL = 10
PIECES = 4
ROW = 8
MSG = FIELDS + 1
MESH = pl.DeviceIdType.MESH


def window(
    n_lon, n_lat, n_comp, levels,
    state, count, rate, flux, weight, target, slot, val, bt_ref,
    raw, cnt, rt, fx, wt, tg, sl,
    grid_q, north_send, row_e, row_w, halo_e, halo_w, halo_n, halo_s, merged,
    part, outbox, inbox, force,
    c0_ref, ib_ref, ab_ref, bb_ref, it_ref, at_ref,
    in_sem, halo_send_sem, halo_recv_sem, msg_sem, column_sem,
):
    per = levels // CHUNKS
    me = lax.axis_index("lon")
    depth = lax.axis_index("lat") * n_comp + lax.axis_index("comp")
    total = n_lat * n_comp
    east = lax.rem(me + 1, n_lon)
    west = lax.rem(me + n_lon - 1, n_lon)
    north = jnp.minimum(depth + 1, total - 1)
    south = jnp.maximum(depth - 1, 0)

    def lon_id(where):
        return {"lon": where}

    def lat_id(where):
        return {"lat": where // n_comp, "comp": lax.rem(where, n_comp)}

    barrier = pltpu.get_barrier_semaphore()
    has_north, has_south = depth < total - 1, depth > 0

    @pl.when(has_north)
    def _():
        pl.semaphore_signal(barrier, inc=1, device_id=lat_id(north), device_id_type=MESH)

    @pl.when(has_south)
    def _():
        pl.semaphore_signal(barrier, inc=1, device_id=lat_id(south), device_id_type=MESH)

    wide = min(ROW, n_lon)
    tall = n_lon // wide
    place = lax.rem(me, wide)
    base = me - place

    def greet(sem, where):
        pl.semaphore_signal(sem, inc=1, device_id=lon_id(where), device_id_type=MESH)

    def greet_row(sem):
        def one(d, carry):
            greet(sem, base + lax.rem(place + d, wide))
            return carry

        lax.fori_loop(1, wide, one, 0)

    ends_row, starts_row = place == wide - 1, place == 0
    if tall > 1:

        @pl.when(ends_row)
        def _():
            greet(barrier, east)

        @pl.when(starts_row)
        def _():
            greet(barrier, west)

        for d in range(1, tall):
            greet(barrier, lax.rem(me + d * wide, n_lon))
    greet_row(barrier)

    @pl.when(jnp.logical_not(has_north))
    def _():
        halo_n[...] = jnp.zeros_like(halo_n)

    @pl.when(jnp.logical_not(has_south))
    def _():
        halo_s[...] = jnp.zeros_like(halo_s)

    cnt_in = pltpu.make_async_copy(count, cnt, in_sem.at[0])
    cnt_in.start()
    raw_in = []
    for c in range(CHUNKS):
        copy = pltpu.make_async_copy(
            state.at[:, pl.ds(c * per, per)], raw.at[:, pl.ds(c * per, per)], in_sem.at[1 + c]
        )
        copy.start()
        raw_in.append(copy)
    lane = lax.broadcasted_iota(jnp.int32, (ROWS, LANES), 1)
    row = lax.broadcasted_iota(jnp.int32, (ROWS, LANES), 0)
    first_lane, last_lane = lane == 0, lane == LANES - 1
    first_row, last_row = row == 0, row == ROWS - 1
    lane_half = lane // 2
    zero = jnp.zeros((ROWS, LANES), jnp.float32)

    def halo_copies(step, c):
        lo = ROWS + c * FIELDS * per
        size = FIELDS * per
        if step == 0 and c == 0:
            lo, size = 0, size + ROWS
        rows = pl.ds(lo, size)
        made = []
        for i, (src, dst, where) in enumerate((
            (row_e.at[step, rows], halo_w.at[step, rows], lon_id(east)),
            (row_w.at[step, rows], halo_e.at[step, rows], lon_id(west)),
            (north_send.at[step, c], halo_s.at[step, c], lat_id(north)),
            (north_send.at[step, c], halo_n.at[step, c], lat_id(south)),
        )):
            made.append(pltpu.make_async_remote_copy(
                src_ref=src,
                dst_ref=dst,
                send_sem=halo_send_sem.at[step, c, i],
                recv_sem=halo_recv_sem.at[step, c, i],
                device_id=where,
                device_id_type=MESH,
            ))
        return made

    def on_sides(made, act):
        act(made[0])
        act(made[1])

        @pl.when(has_north)
        def _():
            act(made[2])

        @pl.when(has_south)
        def _():
            act(made[3])

    def send_halos(step, c):
        on_sides(halo_copies(step, c), lambda copy: copy.start())

    def pack(step, c, kk, fields, packed):
        at = ROWS + (c * per + kk) * FIELDS
        made = []
        for f in range(FIELDS):
            q = fields[f]
            base = ROWS + ((c * per + kk) * FIELDS + f) * ROWS
            grid_q[step, pl.ds(pl.multiple_of(base, ROWS), ROWS), :] = q
            row_w[step, pl.ds(at + f, 1), :] = q[0:1, :]
            row_e[step, pl.ds(at + f, 1), :] = q[ROWS - 1:ROWS, :]
            turned = pltpu.roll(q, 2 * kk + 1, 1)
            made.append(jnp.where(lane_half == kk, turned, packed[f]))
        return tuple(made)

    rest_in = []
    for i, (a, b) in enumerate(((target, tg), (slot, sl), (flux, fx), (weight, wt), (rate, rt))):
        copy = pltpu.make_async_copy(a, b, in_sem.at[1 + CHUNKS + i])
        copy.start()
        rest_in.append(copy)

    cnt_in.wait()
    wet_count = cnt[...]
    wet_count_f = wet_count.astype(jnp.float32)
    for step in range(2):
        grid_q[step, pl.ds(0, ROWS), :] = zero
        grid_q[step, pl.ds(ROWS + levels * FIELDS * ROWS, ROWS), :] = zero
    row_w[0, pl.ds(0, ROWS), :] = jnp.broadcast_to(wet_count_f[0:1, :], (ROWS, LANES))
    row_e[0, pl.ds(0, ROWS), :] = jnp.broadcast_to(wet_count_f[ROWS - 1:, :], (ROWS, LANES))
    for c in range(CHUNKS):
        raw_in[c].wait()

        def pack_raw(kk, packed):
            k = c * per + kk
            wet = k < wet_count
            fields = [jnp.where(wet, raw[f, k], zero) for f in range(FIELDS)]
            return pack(0, c, kk, fields, packed)

        packed = lax.fori_loop(0, per, pack_raw, (zero,) * FIELDS, unroll=UNROLL)
        for f in range(FIELDS):
            tile = packed[f]
            if c == 0 and f == 0:
                turned = pltpu.roll(wet_count_f, 2 * per + 1, 1)
                tile = jnp.where(lane_half == per, turned, tile)
            north_send[0, c, f] = tile
        if c == 0:
            met = wide - 1 + has_north.astype(jnp.int32) + has_south.astype(jnp.int32)
            if tall > 1:
                met = met + tall - 1 + ends_row.astype(jnp.int32) + starts_row.astype(jnp.int32)
            pl.semaphore_wait(barrier, met)
            greet_row(column_sem)
        send_halos(0, c)

    rest_in[0].wait()
    rest_in[1].wait()
    rest_in[2].wait()
    rest_in[3].wait()

    def one_block(b, carry):
        part[b] = jnp.dot(fx[b], wt[b], preferred_element_type=jnp.float32)
        return carry

    lax.fori_loop(0, n_lon, one_block, 0, unroll=16)
    chosen = (
        lax.broadcasted_iota(jnp.int32, (n_lon, n_lon), 0)
        == jnp.broadcast_to(tg[...], (n_lon, n_lon))
    )
    pick = jnp.where(chosen, 1.0, 0.0)
    slot_f = jnp.where(chosen, jnp.broadcast_to(sl[...].astype(jnp.float32), (n_lon, n_lon)), 0.0)
    half = jnp.bfloat16
    pick3 = jnp.concatenate([pick, pick, pick], axis=1).astype(half)
    for f in range(FIELDS):
        whole = part[:, f, :]
        high = whole.astype(half)
        rest = whole - high.astype(jnp.float32)
        middle = rest.astype(half)
        low = (rest - middle.astype(jnp.float32)).astype(half)
        outbox[:, f, :] = jnp.dot(
            pick3, jnp.concatenate([high, middle, low], axis=0),
            preferred_element_type=jnp.float32,
        )
    outbox[:, FIELDS, :] = jnp.broadcast_to(
        jnp.sum(slot_f, axis=1, keepdims=True), (n_lon, LANES)
    )

    def post(d, carry):
        owner = lax.rem(me + d, n_lon)
        pltpu.make_async_remote_copy(
            src_ref=outbox.at[owner],
            dst_ref=inbox.at[me],
            send_sem=msg_sem.at[0],
            recv_sem=msg_sem.at[1],
            device_id=lon_id(owner),
            device_id_type=MESH,
        ).start()
        return carry

    pl.semaphore_wait(column_sem, wide - 1)
    lax.fori_loop(1, n_lon, post, 0)

    rest_in[4].wait()

    def across(k):
        return jnp.where(k + 1 < wet_count, rt[k], zero)

    def factor(i, carry):
        below, inv_b, above, inv_t = carry
        k = levels - 1 - i
        upper = across(jnp.maximum(k - 1, 0))
        upper = jnp.where(k > 0, upper, 0.0)
        inv_b = 1.0 / (1.0 + upper + below - below * below * inv_b)
        masked = jnp.where(k < wet_count, inv_b, 0.0)
        ib_ref[k] = masked
        ab_ref[k] = below * masked
        bb_ref[k] = jnp.where(k > 0, upper, 1.0) * masked
        lower = jnp.where(i < levels - 1, across(i), 0.0)
        inv_t = 1.0 / (1.0 + above + lower - above * above * inv_t)
        masked = jnp.where(i < wet_count, inv_t, 0.0)
        it_ref[i] = masked
        at_ref[i] = jnp.where(i > 0, above, 1.0) * masked
        bt_ref[i] = lower * masked
        return upper, inv_b, lower, inv_t

    lax.fori_loop(0, levels, factor, (zero,) * 4, unroll=UNROLL)

    odd = lax.rem(lane, 2) == 1

    def arrive(step, c):
        made = halo_copies(step, c)
        made[0].wait_recv()
        made[1].wait_recv()

        @pl.when(has_south)
        def _():
            made[2].wait_recv()

        @pl.when(has_north)
        def _():
            made[3].wait_recv()

        for f in range(FIELDS):
            merged[f] = jnp.where(odd, halo_n[step, c, f], halo_s[step, c, f])

    def lat_pair(q, tile, kk):
        edge = pltpu.roll(tile, LANES - 1 - 2 * kk, 1)
        n = pltpu.roll(jnp.where(first_lane, edge, q), LANES - 1, 1)
        s = pltpu.roll(jnp.where(last_lane, edge, q), 1, 1)
        return n, s

    def row_of(ref, step, at):
        return jnp.broadcast_to(ref[step, pl.ds(at, 1), :], (ROWS, LANES))

    y = (depth * LANES + lane).astype(jnp.float32)
    turning = CORIOLIS * (2.0 * (y + 0.5) / (total * LANES) - 1.0)

    def tendency(step, c, kk, sums, counts):
        k = c * per + kk
        at = ROWS + k * FIELDS
        mid, e, w, n, s = [], [], [], [], []
        for f in range(FIELDS):
            base = ROWS + (k * FIELDS + f) * ROWS
            q = grid_q[step, pl.ds(pl.multiple_of(base, ROWS), ROWS), :]
            e.append(jnp.where(last_row, row_of(halo_e, step, at + f), pltpu.roll(q, ROWS - 1, 0)))
            w.append(jnp.where(first_row, row_of(halo_w, step, at + f), pltpu.roll(q, 1, 0)))
            up, down = lat_pair(q, merged[f], kk)
            n.append(up)
            s.append(down)
            mid.append(q)
        wets = [k < a for a in counts]
        if step == 0:
            shares = [jnp.where(m, DIFFUSE, 0.0) for m in wets]
            c0 = (1.0 - (shares[0] + shares[1])) - (shares[2] + shares[3])
            c0_ref[k] = c0
        else:
            c0 = c0_ref[k]
        half = 0.5 * ADVECTION
        a, b = half * mid[2], half * mid[3]
        to_e, to_w, to_n, to_s = DIFFUSE - a, DIFFUSE + a, DIFFUSE - b, DIFFUSE + b
        new = []
        for f in range(2):
            new.append(
                c0 * mid[f]
                + ((to_e * e[f] + to_w * w[f]) + (to_n * n[f] + to_s * s[f]))
            )
        scale = 0.5 * GRAVITY
        made, pressures = [], []
        for side, m, total_d in zip((e, w, n, s), wets, sums):
            total_d = total_d + (scale * HALINE * side[1] - scale * THERMAL * side[0])
            made.append(total_d)
            pressures.append(jnp.where(m, total_d, 0.0))
        for f, sign, lo, hi in ((2, 1, 1, 0), (3, -1, 3, 2)):
            spread = DIFFUSE * ((e[f] + w[f]) + (n[f] + s[f]))
            twist = turning * mid[5 - f]
            base = c0 * mid[f] + spread
            base = base + twist if sign > 0 else base - twist
            new.append(base - (pressures[hi] - pressures[lo]))
        return new, tuple(made)

    arrive(0, 0)
    count_e = jnp.where(last_row, halo_e[0, pl.ds(0, ROWS), :], pltpu.roll(wet_count_f, ROWS - 1, 0))
    count_w = jnp.where(first_row, halo_w[0, pl.ds(0, ROWS), :], pltpu.roll(wet_count_f, 1, 0))
    count_n, count_s = lat_pair(wet_count_f, merged[0], per)
    counts = [a.astype(jnp.int32) for a in (count_e, count_w, count_n, count_s)]
    sums = (zero,) * 4
    for c in range(CHUNKS):
        if c > 0:
            arrive(0, c)

        def first(kk, sums):
            new, sums = tendency(0, c, kk, sums, counts)
            k = c * per + kk
            ib = ib_ref[k]
            for f in range(FIELDS):
                val[k, f] = ib * new[f]
            return sums

        sums = lax.fori_loop(0, per, first, sums, unroll=UNROLL)

    def upward(i, carry):
        k = levels - 1 - i
        ab = ab_ref[k]
        made = tuple(val[k, f] + ab * carry[f] for f in range(FIELDS))
        for f in range(FIELDS):
            val[k, f] = made[f]
        return made

    lax.fori_loop(0, levels, upward, (zero,) * FIELDS, unroll=UNROLL)

    inbox[me] = outbox[me]
    pltpu.make_async_copy(
        inbox.at[pl.ds(0, n_lon - 1)], inbox.at[pl.ds(0, n_lon - 1)], msg_sem.at[1]
    ).wait()
    row_f = row.astype(jnp.float32)

    def receive(s, carry):
        hit = row_f == jnp.broadcast_to(inbox[s, pl.ds(FIELDS, 1), :], (ROWS, LANES))
        return tuple(
            carry[f]
            + jnp.where(hit, jnp.broadcast_to(inbox[s, pl.ds(f, 1), :], (ROWS, LANES)), 0.0)
            for f in range(FIELDS)
        )

    forced = lax.fori_loop(0, n_lon, receive, (zero,) * FIELDS, unroll=UNROLL)
    for f in range(FIELDS):
        force[f] = SURFACE_GAIN[f] * forced[f]

    carry = tuple(force[f] for f in range(FIELDS))
    for c in range(CHUNKS):

        def downward(kk, carry):
            before, packed = carry
            k = c * per + kk
            bb = bb_ref[k]
            made = tuple(val[k, f] + bb * before[f] for f in range(FIELDS))
            return made, pack(1, c, kk, made, packed)

        carry, packed = lax.fori_loop(0, per, downward, (carry, (zero,) * FIELDS), unroll=UNROLL)
        for f in range(FIELDS):
            north_send[1, c, f] = packed[f]
        send_halos(1, c)

    sums = (zero,) * 4
    carry = tuple(force[f] for f in range(FIELDS))
    for c in range(CHUNKS):
        on_sides(halo_copies(0, c), lambda copy: copy.wait_send())
    pltpu.make_async_copy(
        outbox.at[pl.ds(0, n_lon - 1)], outbox.at[pl.ds(0, n_lon - 1)], msg_sem.at[0]
    ).wait()
    for c in range(CHUNKS):
        if c == CHUNKS - 1:
            for sent in range(CHUNKS):
                on_sides(halo_copies(1, sent), lambda copy: copy.wait_send())
        arrive(1, c)

        def second(kk, state_in):
            sums, before = state_in
            new, sums = tendency(1, c, kk, sums, counts)
            k = c * per + kk
            it, at = it_ref[k], at_ref[k]
            made = tuple(it * new[f] + at * before[f] for f in range(FIELDS))
            for f in range(FIELDS):
                val[k, f] = made[f]
            return sums, made

        sums, carry = lax.fori_loop(0, per, second, (sums, carry), unroll=UNROLL)


def finish(levels, val, bt_ref, out, res, sem):
    per = levels // PIECES
    carry = (jnp.zeros((ROWS, LANES), jnp.float32),) * FIELDS
    outs = []
    for c in reversed(range(PIECES)):

        def settle(i, carry):
            k = c * per + per - 1 - i
            bt = bt_ref[k]
            made = tuple(val[k, f] + bt * carry[f] for f in range(FIELDS))
            for f in range(FIELDS):
                res[f, k] = made[f]
            return made

        carry = lax.fori_loop(0, per, settle, carry, unroll=10)
        here = pl.ds(c * per, per)
        copy = pltpu.make_async_copy(res.at[:, here], out.at[:, here], sem.at[c])
        copy.start()
        outs.append(copy)
    for copy in outs:
        copy.wait()


def local(ocean_state, level_count, mix_rate, atmos_flux, remap_weight, remap_target, remap_slot):
    fields, levels, rows, lanes = ocean_state.shape
    n_lon, n_lat, n_comp = (lax.axis_size(a) for a in ("lon", "lat", "comp"))
    blocks, cells = atmos_flux.shape[1], atmos_flux.shape[3]
    per = levels // CHUNKS
    tile = (levels, rows, lanes)
    f32 = jnp.float32
    row_shape = (2, ROWS + levels * fields, lanes)
    lat_shape = (2, CHUNKS, fields, rows, lanes)
    anywhere = pl.BlockSpec(memory_space=pltpu.HBM)
    inside = pl.BlockSpec(memory_space=pltpu.VMEM)
    stack = (levels, fields, rows, lanes)
    val, bt = pl.pallas_call(
        functools.partial(window, n_lon, n_lat, n_comp, levels),
        out_shape=(jax.ShapeDtypeStruct(stack, f32), jax.ShapeDtypeStruct(tile, f32)),
        in_specs=[anywhere] * 7,
        out_specs=(inside, inside),
        scratch_shapes=[
            pltpu.VMEM(ocean_state.shape, f32),
            pltpu.VMEM((rows, lanes), jnp.int32),
            pltpu.VMEM(tile, f32),
            pltpu.VMEM((blocks, fields, cells), jnp.bfloat16),
            pltpu.VMEM((blocks, cells, lanes), jnp.bfloat16),
            pltpu.VMEM((1, blocks), jnp.int32),
            pltpu.VMEM((1, blocks), jnp.int32),
            pltpu.VMEM((2, levels * fields * rows + 2 * rows, lanes), f32),
            pltpu.VMEM(lat_shape, f32),
            pltpu.VMEM(row_shape, f32),
            pltpu.VMEM(row_shape, f32),
            pltpu.VMEM(row_shape, f32),
            pltpu.VMEM(row_shape, f32),
            pltpu.VMEM(lat_shape, f32),
            pltpu.VMEM(lat_shape, f32),
            pltpu.VMEM((fields, rows, lanes), f32),
            pltpu.VMEM((blocks, fields, lanes), f32),
            pltpu.VMEM((n_lon, MSG, lanes), f32),
            pltpu.VMEM((n_lon, MSG, lanes), f32),
            pltpu.VMEM((fields, rows, lanes), f32),
        ]
        + [pltpu.VMEM(tile, f32)] * 6
        + [
            pltpu.SemaphoreType.DMA((1 + CHUNKS + 5,)),
            pltpu.SemaphoreType.DMA((2, CHUNKS, 4)),
            pltpu.SemaphoreType.DMA((2, CHUNKS, 4)),
            pltpu.SemaphoreType.DMA((2,)),
            pltpu.SemaphoreType.REGULAR,
        ],
        compiler_params=pltpu.CompilerParams(
            collective_id=0, has_side_effects=True, vmem_limit_bytes=40 << 20
        ),
        cost_estimate=pl.CostEstimate(flops=20_000_000, bytes_accessed=5_200_000, transcendentals=0),
    )(*(pltpu.with_memory_space_constraint(x, pltpu.HBM) for x in (
        ocean_state, level_count, mix_rate, atmos_flux[0], remap_weight[0], remap_target, remap_slot
    )))

    return pl.pallas_call(
        functools.partial(finish, levels),
        out_shape=jax.ShapeDtypeStruct(ocean_state.shape, f32),
        in_specs=[inside, inside],
        out_specs=anywhere,
        scratch_shapes=[
            pltpu.VMEM(ocean_state.shape, f32),
            pltpu.SemaphoreType.DMA((PIECES,)),
        ],
        compiler_params=pltpu.CompilerParams(vmem_limit_bytes=16 << 20),
        cost_estimate=pl.CostEstimate(flops=700_000, bytes_accessed=3_000_000, transcendentals=0),
    )(val, bt)


def solution(mesh):
    placed = (
        P(None, None, "lon", ("lat", "comp")),
        P("lon", ("lat", "comp")),
        P(None, "lon", ("lat", "comp")),
        P(("lat", "comp"), "lon", None, None),
        P(("lat", "comp"), "lon", None, None),
        P(("lat", "comp"), "lon"),
        P(("lat", "comp"), "lon"),
    )
    return jax.shard_map(
        local,
        mesh=mesh,
        in_specs=placed,
        out_specs=P(None, None, "lon", ("lat", "comp")),
        check_vma=False,
    )
```

```python
import functools

import jax
import jax.numpy as jnp
from jax import lax
from jax.experimental import pallas as pl
from jax.experimental.pallas import tpu as pltpu
from jax.sharding import PartitionSpec as P

DIFFUSE = 0.2
ADVECTION = 0.5
THERMAL = 0.2
HALINE = 0.15
GRAVITY = 0.05
CORIOLIS = 0.3
SURFACE_GAIN = (0.5, 0.4, 0.6, 0.6)

FIELDS = 4
ROWS = 8
LANES = 128
CHUNKS = 4
UNROLL = 10
PIECES = 4
ROW = 8
MSG = FIELDS + 1
MESH = pl.DeviceIdType.MESH


def window(
    n_lon, n_lat, n_comp, levels,
    state, count, rate, flux, weight, target, slot, val, bt_ref,
    raw, cnt, rt, fx, wt, tg, sl,
    grid_q, north_send, row_e, row_w, halo_e, halo_w, halo_n, halo_s, merged,
    part, outbox, inbox, force,
    c0_ref, ib_ref, ab_ref, bb_ref, it_ref, at_ref,
    in_sem, halo_send_sem, halo_recv_sem, msg_sem, column_sem,
):
    per = levels // CHUNKS
    me = lax.axis_index("lon")
    depth = lax.axis_index("lat") * n_comp + lax.axis_index("comp")
    total = n_lat * n_comp
    east = lax.rem(me + 1, n_lon)
    west = lax.rem(me + n_lon - 1, n_lon)
    north = jnp.minimum(depth + 1, total - 1)
    south = jnp.maximum(depth - 1, 0)

    def lon_id(where):
        return {"lon": where}

    def lat_id(where):
        return {"lat": where // n_comp, "comp": lax.rem(where, n_comp)}

    barrier = pltpu.get_barrier_semaphore()
    has_north, has_south = depth < total - 1, depth > 0

    @pl.when(has_north)
    def _():
        pl.semaphore_signal(barrier, inc=1, device_id=lat_id(north), device_id_type=MESH)

    @pl.when(has_south)
    def _():
        pl.semaphore_signal(barrier, inc=1, device_id=lat_id(south), device_id_type=MESH)

    wide = min(ROW, n_lon)
    tall = n_lon // wide
    place = lax.rem(me, wide)
    base = me - place

    def greet(sem, where):
        pl.semaphore_signal(sem, inc=1, device_id=lon_id(where), device_id_type=MESH)

    def greet_row(sem):
        def one(d, carry):
            greet(sem, base + lax.rem(place + d, wide))
            return carry

        lax.fori_loop(1, wide, one, 0)

    ends_row, starts_row = place == wide - 1, place == 0
    if tall > 1:

        @pl.when(ends_row)
        def _():
            greet(barrier, east)

        @pl.when(starts_row)
        def _():
            greet(barrier, west)

        for d in range(1, tall):
            greet(barrier, lax.rem(me + d * wide, n_lon))
    greet_row(barrier)

    @pl.when(jnp.logical_not(has_north))
    def _():
        halo_n[...] = jnp.zeros_like(halo_n)

    @pl.when(jnp.logical_not(has_south))
    def _():
        halo_s[...] = jnp.zeros_like(halo_s)

    cnt_in = pltpu.make_async_copy(count, cnt, in_sem.at[0])
    cnt_in.start()
    raw_in = []
    for c in range(CHUNKS):
        copy = pltpu.make_async_copy(
            state.at[:, pl.ds(c * per, per)], raw.at[:, pl.ds(c * per, per)], in_sem.at[1 + c]
        )
        copy.start()
        raw_in.append(copy)
    lane = lax.broadcasted_iota(jnp.int32, (ROWS, LANES), 1)
    row = lax.broadcasted_iota(jnp.int32, (ROWS, LANES), 0)
    first_lane, last_lane = lane == 0, lane == LANES - 1
    first_row, last_row = row == 0, row == ROWS - 1
    lane_half = lane // 2
    zero = jnp.zeros((ROWS, LANES), jnp.float32)

    def halo_copies(step, c):
        lo = ROWS + c * FIELDS * per
        size = FIELDS * per
        if step == 0 and c == 0:
            lo, size = 0, size + ROWS
        rows = pl.ds(lo, size)
        made = []
        for i, (src, dst, where) in enumerate((
            (row_e.at[step, rows], halo_w.at[step, rows], lon_id(east)),
            (row_w.at[step, rows], halo_e.at[step, rows], lon_id(west)),
            (north_send.at[step, c], halo_s.at[step, c], lat_id(north)),
            (north_send.at[step, c], halo_n.at[step, c], lat_id(south)),
        )):
            made.append(pltpu.make_async_remote_copy(
                src_ref=src,
                dst_ref=dst,
                send_sem=halo_send_sem.at[step, c, i],
                recv_sem=halo_recv_sem.at[step, c, i],
                device_id=where,
                device_id_type=MESH,
            ))
        return made

    def on_sides(made, act):
        act(made[0])
        act(made[1])

        @pl.when(has_north)
        def _():
            act(made[2])

        @pl.when(has_south)
        def _():
            act(made[3])

    def send_halos(step, c):
        on_sides(halo_copies(step, c), lambda copy: copy.start())

    def pack(step, c, kk, fields, packed):
        at = ROWS + (c * per + kk) * FIELDS
        made = []
        for f in range(FIELDS):
            q = fields[f]
            base = ROWS + ((c * per + kk) * FIELDS + f) * ROWS
            grid_q[step, pl.ds(pl.multiple_of(base, ROWS), ROWS), :] = q
            row_w[step, pl.ds(at + f, 1), :] = q[0:1, :]
            row_e[step, pl.ds(at + f, 1), :] = q[ROWS - 1:ROWS, :]
            turned = pltpu.roll(q, 2 * kk + 1, 1)
            made.append(jnp.where(lane_half == kk, turned, packed[f]))
        return tuple(made)

    rest_in = []
    for i, (a, b) in enumerate(((target, tg), (slot, sl), (flux, fx), (weight, wt), (rate, rt))):
        copy = pltpu.make_async_copy(a, b, in_sem.at[1 + CHUNKS + i])
        copy.start()
        rest_in.append(copy)

    cnt_in.wait()
    wet_count = cnt[...]
    wet_count_f = wet_count.astype(jnp.float32)
    for step in range(2):
        grid_q[step, pl.ds(0, ROWS), :] = zero
        grid_q[step, pl.ds(ROWS + levels * FIELDS * ROWS, ROWS), :] = zero
    row_w[0, pl.ds(0, ROWS), :] = jnp.broadcast_to(wet_count_f[0:1, :], (ROWS, LANES))
    row_e[0, pl.ds(0, ROWS), :] = jnp.broadcast_to(wet_count_f[ROWS - 1:, :], (ROWS, LANES))
    for c in range(CHUNKS):
        raw_in[c].wait()

        def pack_raw(kk, packed):
            k = c * per + kk
            wet = k < wet_count
            fields = [jnp.where(wet, raw[f, k], zero) for f in range(FIELDS)]
            return pack(0, c, kk, fields, packed)

        packed = lax.fori_loop(0, per, pack_raw, (zero,) * FIELDS, unroll=UNROLL)
        for f in range(FIELDS):
            tile = packed[f]
            if c == 0 and f == 0:
                turned = pltpu.roll(wet_count_f, 2 * per + 1, 1)
                tile = jnp.where(lane_half == per, turned, tile)
            north_send[0, c, f] = tile
        if c == 0:
            met = wide - 1 + has_north.astype(jnp.int32) + has_south.astype(jnp.int32)
            if tall > 1:
                met = met + tall - 1 + ends_row.astype(jnp.int32) + starts_row.astype(jnp.int32)
            pl.semaphore_wait(barrier, met)
        send_halos(0, c)
        if c == 0:
            greet_row(column_sem)

    rest_in[0].wait()
    rest_in[1].wait()
    rest_in[2].wait()
    rest_in[3].wait()

    def one_block(b, carry):
        part[b] = jnp.dot(fx[b], wt[b], preferred_element_type=jnp.float32)
        return carry

    lax.fori_loop(0, n_lon, one_block, 0, unroll=16)
    chosen = (
        lax.broadcasted_iota(jnp.int32, (n_lon, n_lon), 0)
        == jnp.broadcast_to(tg[...], (n_lon, n_lon))
    )
    pick = jnp.where(chosen, 1.0, 0.0)
    slot_f = jnp.where(chosen, jnp.broadcast_to(sl[...].astype(jnp.float32), (n_lon, n_lon)), 0.0)
    half = jnp.bfloat16
    pick3 = jnp.concatenate([pick, pick, pick], axis=1).astype(half)
    for f in range(FIELDS):
        whole = part[:, f, :]
        high = whole.astype(half)
        rest = whole - high.astype(jnp.float32)
        middle = rest.astype(half)
        low = (rest - middle.astype(jnp.float32)).astype(half)
        outbox[:, f, :] = jnp.dot(
            pick3, jnp.concatenate([high, middle, low], axis=0),
            preferred_element_type=jnp.float32,
        )
    outbox[:, FIELDS, :] = jnp.broadcast_to(
        jnp.sum(slot_f, axis=1, keepdims=True), (n_lon, LANES)
    )

    def post(d, carry):
        owner = lax.rem(me + d, n_lon)
        pltpu.make_async_remote_copy(
            src_ref=outbox.at[owner],
            dst_ref=inbox.at[me],
            send_sem=msg_sem.at[0],
            recv_sem=msg_sem.at[1],
            device_id=lon_id(owner),
            device_id_type=MESH,
        ).start()
        return carry

    pl.semaphore_wait(column_sem, wide - 1)
    lax.fori_loop(1, n_lon, post, 0)

    rest_in[4].wait()

    def across(k):
        return jnp.where(k + 1 < wet_count, rt[k], zero)

    def factor(i, carry):
        below, inv_b, above, inv_t = carry
        k = levels - 1 - i
        upper = across(jnp.maximum(k - 1, 0))
        upper = jnp.where(k > 0, upper, 0.0)
        inv_b = 1.0 / (1.0 + upper + below - below * below * inv_b)
        masked = jnp.where(k < wet_count, inv_b, 0.0)
        ib_ref[k] = masked
        ab_ref[k] = below * masked
        bb_ref[k] = jnp.where(k > 0, upper, 1.0) * masked
        lower = jnp.where(i < levels - 1, across(i), 0.0)
        inv_t = 1.0 / (1.0 + above + lower - above * above * inv_t)
        masked = jnp.where(i < wet_count, inv_t, 0.0)
        it_ref[i] = masked
        at_ref[i] = jnp.where(i > 0, above, 1.0) * masked
        bt_ref[i] = lower * masked
        return upper, inv_b, lower, inv_t

    lax.fori_loop(0, levels, factor, (zero,) * 4, unroll=UNROLL)

    odd = lax.rem(lane, 2) == 1

    def arrive(step, c):
        made = halo_copies(step, c)
        made[0].wait_recv()
        made[1].wait_recv()

        @pl.when(has_south)
        def _():
            made[2].wait_recv()

        @pl.when(has_north)
        def _():
            made[3].wait_recv()

        for f in range(FIELDS):
            merged[f] = jnp.where(odd, halo_n[step, c, f], halo_s[step, c, f])

    def lat_pair(q, tile, kk):
        edge = pltpu.roll(tile, LANES - 1 - 2 * kk, 1)
        n = pltpu.roll(jnp.where(first_lane, edge, q), LANES - 1, 1)
        s = pltpu.roll(jnp.where(last_lane, edge, q), 1, 1)
        return n, s

    def row_of(ref, step, at):
        return jnp.broadcast_to(ref[step, pl.ds(at, 1), :], (ROWS, LANES))

    y = (depth * LANES + lane).astype(jnp.float32)
    turning = CORIOLIS * (2.0 * (y + 0.5) / (total * LANES) - 1.0)

    def tendency(step, c, kk, sums, counts):
        k = c * per + kk
        at = ROWS + k * FIELDS
        mid, e, w, n, s = [], [], [], [], []
        for f in range(FIELDS):
            base = ROWS + (k * FIELDS + f) * ROWS
            q = grid_q[step, pl.ds(pl.multiple_of(base, ROWS), ROWS), :]
            e.append(jnp.where(last_row, row_of(halo_e, step, at + f), pltpu.roll(q, ROWS - 1, 0)))
            w.append(jnp.where(first_row, row_of(halo_w, step, at + f), pltpu.roll(q, 1, 0)))
            up, down = lat_pair(q, merged[f], kk)
            n.append(up)
            s.append(down)
            mid.append(q)
        wets = [k < a for a in counts]
        if step == 0:
            shares = [jnp.where(m, DIFFUSE, 0.0) for m in wets]
            c0 = (1.0 - (shares[0] + shares[1])) - (shares[2] + shares[3])
            c0_ref[k] = c0
        else:
            c0 = c0_ref[k]
        half = 0.5 * ADVECTION
        a, b = half * mid[2], half * mid[3]
        to_e, to_w, to_n, to_s = DIFFUSE - a, DIFFUSE + a, DIFFUSE - b, DIFFUSE + b
        new = []
        for f in range(2):
            new.append(
                c0 * mid[f]
                + ((to_e * e[f] + to_w * w[f]) + (to_n * n[f] + to_s * s[f]))
            )
        scale = 0.5 * GRAVITY
        made, pressures = [], []
        for side, m, total_d in zip((e, w, n, s), wets, sums):
            total_d = total_d + (scale * HALINE * side[1] - scale * THERMAL * side[0])
            made.append(total_d)
            pressures.append(jnp.where(m, total_d, 0.0))
        for f, sign, lo, hi in ((2, 1, 1, 0), (3, -1, 3, 2)):
            spread = DIFFUSE * ((e[f] + w[f]) + (n[f] + s[f]))
            twist = turning * mid[5 - f]
            base = c0 * mid[f] + spread
            base = base + twist if sign > 0 else base - twist
            new.append(base - (pressures[hi] - pressures[lo]))
        return new, tuple(made)

    arrive(0, 0)
    count_e = jnp.where(last_row, halo_e[0, pl.ds(0, ROWS), :], pltpu.roll(wet_count_f, ROWS - 1, 0))
    count_w = jnp.where(first_row, halo_w[0, pl.ds(0, ROWS), :], pltpu.roll(wet_count_f, 1, 0))
    count_n, count_s = lat_pair(wet_count_f, merged[0], per)
    counts = [a.astype(jnp.int32) for a in (count_e, count_w, count_n, count_s)]
    sums = (zero,) * 4
    for c in range(CHUNKS):
        if c > 0:
            arrive(0, c)

        def first(kk, sums):
            new, sums = tendency(0, c, kk, sums, counts)
            k = c * per + kk
            ib = ib_ref[k]
            for f in range(FIELDS):
                val[k, f] = ib * new[f]
            return sums

        sums = lax.fori_loop(0, per, first, sums, unroll=UNROLL)

    def upward(i, carry):
        k = levels - 1 - i
        ab = ab_ref[k]
        made = tuple(val[k, f] + ab * carry[f] for f in range(FIELDS))
        for f in range(FIELDS):
            val[k, f] = made[f]
        return made

    lax.fori_loop(0, levels, upward, (zero,) * FIELDS, unroll=UNROLL)

    inbox[me] = outbox[me]
    pltpu.make_async_copy(
        inbox.at[pl.ds(0, n_lon - 1)], inbox.at[pl.ds(0, n_lon - 1)], msg_sem.at[1]
    ).wait()
    row_f = row.astype(jnp.float32)

    def receive(s, carry):
        hit = row_f == jnp.broadcast_to(inbox[s, pl.ds(FIELDS, 1), :], (ROWS, LANES))
        return tuple(
            carry[f]
            + jnp.where(hit, jnp.broadcast_to(inbox[s, pl.ds(f, 1), :], (ROWS, LANES)), 0.0)
            for f in range(FIELDS)
        )

    forced = lax.fori_loop(0, n_lon, receive, (zero,) * FIELDS, unroll=UNROLL)
    for f in range(FIELDS):
        force[f] = SURFACE_GAIN[f] * forced[f]

    carry = tuple(force[f] for f in range(FIELDS))
    for c in range(CHUNKS):

        def downward(kk, carry):
            before, packed = carry
            k = c * per + kk
            bb = bb_ref[k]
            made = tuple(val[k, f] + bb * before[f] for f in range(FIELDS))
            return made, pack(1, c, kk, made, packed)

        carry, packed = lax.fori_loop(0, per, downward, (carry, (zero,) * FIELDS), unroll=UNROLL)
        for f in range(FIELDS):
            north_send[1, c, f] = packed[f]
        send_halos(1, c)

    sums = (zero,) * 4
    carry = tuple(force[f] for f in range(FIELDS))
    for c in range(CHUNKS):
        on_sides(halo_copies(0, c), lambda copy: copy.wait_send())
    pltpu.make_async_copy(
        outbox.at[pl.ds(0, n_lon - 1)], outbox.at[pl.ds(0, n_lon - 1)], msg_sem.at[0]
    ).wait()
    for c in range(CHUNKS):
        if c == CHUNKS - 1:
            for sent in range(CHUNKS):
                on_sides(halo_copies(1, sent), lambda copy: copy.wait_send())
        arrive(1, c)

        def second(kk, state_in):
            sums, before = state_in
            new, sums = tendency(1, c, kk, sums, counts)
            k = c * per + kk
            it, at = it_ref[k], at_ref[k]
            made = tuple(it * new[f] + at * before[f] for f in range(FIELDS))
            for f in range(FIELDS):
                val[k, f] = made[f]
            return sums, made

        sums, carry = lax.fori_loop(0, per, second, (sums, carry), unroll=UNROLL)


def finish(levels, val, bt_ref, out, res, sem):
    per = levels // PIECES
    carry = (jnp.zeros((ROWS, LANES), jnp.float32),) * FIELDS
    outs = []
    for c in reversed(range(PIECES)):

        def settle(i, carry):
            k = c * per + per - 1 - i
            bt = bt_ref[k]
            made = tuple(val[k, f] + bt * carry[f] for f in range(FIELDS))
            for f in range(FIELDS):
                res[f, k] = made[f]
            return made

        carry = lax.fori_loop(0, per, settle, carry, unroll=10)
        here = pl.ds(c * per, per)
        copy = pltpu.make_async_copy(res.at[:, here], out.at[:, here], sem.at[c])
        copy.start()
        outs.append(copy)
    for copy in outs:
        copy.wait()


def local(ocean_state, level_count, mix_rate, atmos_flux, remap_weight, remap_target, remap_slot):
    fields, levels, rows, lanes = ocean_state.shape
    n_lon, n_lat, n_comp = (lax.axis_size(a) for a in ("lon", "lat", "comp"))
    blocks, cells = atmos_flux.shape[1], atmos_flux.shape[3]
    per = levels // CHUNKS
    tile = (levels, rows, lanes)
    f32 = jnp.float32
    row_shape = (2, ROWS + levels * fields, lanes)
    lat_shape = (2, CHUNKS, fields, rows, lanes)
    anywhere = pl.BlockSpec(memory_space=pltpu.HBM)
    inside = pl.BlockSpec(memory_space=pltpu.VMEM)
    stack = (levels, fields, rows, lanes)
    val, bt = pl.pallas_call(
        functools.partial(window, n_lon, n_lat, n_comp, levels),
        out_shape=(jax.ShapeDtypeStruct(stack, f32), jax.ShapeDtypeStruct(tile, f32)),
        in_specs=[anywhere] * 7,
        out_specs=(inside, inside),
        scratch_shapes=[
            pltpu.VMEM(ocean_state.shape, f32),
            pltpu.VMEM((rows, lanes), jnp.int32),
            pltpu.VMEM(tile, f32),
            pltpu.VMEM((blocks, fields, cells), jnp.bfloat16),
            pltpu.VMEM((blocks, cells, lanes), jnp.bfloat16),
            pltpu.VMEM((1, blocks), jnp.int32),
            pltpu.VMEM((1, blocks), jnp.int32),
            pltpu.VMEM((2, levels * fields * rows + 2 * rows, lanes), f32),
            pltpu.VMEM(lat_shape, f32),
            pltpu.VMEM(row_shape, f32),
            pltpu.VMEM(row_shape, f32),
            pltpu.VMEM(row_shape, f32),
            pltpu.VMEM(row_shape, f32),
            pltpu.VMEM(lat_shape, f32),
            pltpu.VMEM(lat_shape, f32),
            pltpu.VMEM((fields, rows, lanes), f32),
            pltpu.VMEM((blocks, fields, lanes), f32),
            pltpu.VMEM((n_lon, MSG, lanes), f32),
            pltpu.VMEM((n_lon, MSG, lanes), f32),
            pltpu.VMEM((fields, rows, lanes), f32),
        ]
        + [pltpu.VMEM(tile, f32)] * 6
        + [
            pltpu.SemaphoreType.DMA((1 + CHUNKS + 5,)),
            pltpu.SemaphoreType.DMA((2, CHUNKS, 4)),
            pltpu.SemaphoreType.DMA((2, CHUNKS, 4)),
            pltpu.SemaphoreType.DMA((2,)),
            pltpu.SemaphoreType.REGULAR,
        ],
        compiler_params=pltpu.CompilerParams(
            collective_id=0, has_side_effects=True, vmem_limit_bytes=40 << 20
        ),
        cost_estimate=pl.CostEstimate(flops=20_000_000, bytes_accessed=5_200_000, transcendentals=0),
    )(*(pltpu.with_memory_space_constraint(x, pltpu.HBM) for x in (
        ocean_state, level_count, mix_rate, atmos_flux[0], remap_weight[0], remap_target, remap_slot
    )))

    return pl.pallas_call(
        functools.partial(finish, levels),
        out_shape=jax.ShapeDtypeStruct(ocean_state.shape, f32),
        in_specs=[inside, inside],
        out_specs=anywhere,
        scratch_shapes=[
            pltpu.VMEM(ocean_state.shape, f32),
            pltpu.SemaphoreType.DMA((PIECES,)),
        ],
        compiler_params=pltpu.CompilerParams(vmem_limit_bytes=16 << 20),
        cost_estimate=pl.CostEstimate(flops=700_000, bytes_accessed=3_000_000, transcendentals=0),
    )(val, bt)


def solution(mesh):
    placed = (
        P(None, None, "lon", ("lat", "comp")),
        P("lon", ("lat", "comp")),
        P(None, "lon", ("lat", "comp")),
        P(("lat", "comp"), "lon", None, None),
        P(("lat", "comp"), "lon", None, None),
        P(("lat", "comp"), "lon"),
        P(("lat", "comp"), "lon"),
    )
    return jax.shard_map(
        local,
        mesh=mesh,
        in_specs=placed,
        out_specs=P(None, None, "lon", ("lat", "comp")),
        check_vma=False,
    )
```
